256 devices in a mesh: pulse: 16 (over z, core), sample: 16 (over y, x).
Axes of the slice: x: 4, y: 4, z: 8, core: 2. Of those that a mesh axis runs over, the one named last changes fastest.
Arguments:
- echoes: bfloat16 [16384, 32768], P('pulse', 'sample'), may hold values from -40 to 40
- chirp_phase: float32 [16384], replicated, may hold values from -3.140625 to 3.140625
- sample_init: bfloat16 [32768, 64], P('sample'), may hold values from -0.03125 to 0.03125
- threshold: float32 [1], replicated, may hold values from 1 to 2
- ridge_scale: float32 [1], replicated, may hold values from 0.05 to 0.5
Outputs:
- doppler: float32 [256, 2, 32768], P('pulse', None, 'sample')
- rfi_pulses: float32 [16384, 64], P('pulse')
- sparse: bfloat16 [16384, 32768], P('pulse', 'sample')
The draws below stay inside these ranges and needn't reach their ends.
All inputs are finite; a program needn't handle non-finite values.
Results may differ from the reference program's by a relative error of at most 0.0075.
Values may be sent and summed in bfloat16 or wider, within the bound.
No kernel may reach another device: no remote copies, remote signals or barrier semaphores. Data moves between devices by JAX's collectives and lax.ppermute only.
A program may use at most 64 MiB of HBM per device.

```python
import math
import jax
import jax.numpy as jnp

S_DEV = 2048
RANK = 64
BINS = 256
ITERS = 2
PULSES = 16384
SAMPLES = 32768


tone_count = 8


period_cells = 4096


def tone_field(key):
    key_freq, key_amp, key_env, key_phase, key_group = jax.random.split(key, 5)
    groups = SAMPLES // S_DEV
    order = jax.random.permutation(key_group, groups)
    chosen = (order < (groups + 1) // 2).astype(jnp.float32)
    column_mask = jnp.repeat(chosen, S_DEV).reshape(1, SAMPLES)
    steps_int = jax.random.randint(key_freq, (tone_count,), 80, 1840).astype(jnp.int32)
    amplitude = jnp.exp(jax.random.uniform(key_amp, (tone_count,), jnp.float32, math.log(0.8), math.log(1.6)))
    envelope = jax.random.uniform(key_env, (PULSES, tone_count), jnp.float32, 0.6, 1.4) * amplitude[None, :]
    phase = jax.random.uniform(key_phase, (PULSES, tone_count), jnp.float32, -math.pi, math.pi)
    along_cos = envelope * jnp.cos(phase)
    along_sin = envelope * jnp.sin(phase)
    samples = jnp.arange(SAMPLES, dtype=jnp.int32)
    field = jnp.zeros((PULSES, SAMPLES), jnp.float32)
    for tone in range(tone_count):
        index = jnp.mod(steps_int[tone] * samples, period_cells).astype(jnp.int32)
        angle = 2.0 * math.pi * index.astype(jnp.float32) / period_cells
        field = field + along_cos[:, tone:tone + 1] * jnp.cos(angle)[None, :]
        field = field - along_sin[:, tone:tone + 1] * jnp.sin(angle)[None, :]
    return field * column_mask


def draw_echoes(key, part):
    key_rows, key_cols, key_noise, key_tone = jax.random.split(jax.random.fold_in(key, 17), 4)
    position = jnp.arange(PULSES, dtype=jnp.float32).reshape(PULSES, 1) / (PULSES - 1)
    col_scale = jnp.exp(jax.random.uniform(key_cols, (1, SAMPLES), jnp.float32, -1.15, 1.15))
    trend = -0.8 + 1.6 * position
    row_scale = jnp.exp(trend + jax.random.uniform(key_rows, (PULSES, 1), jnp.float32, -0.35, 0.35))
    noise = jnp.clip(jax.random.normal(key_noise, (PULSES, SAMPLES), jnp.float32), -3.9, 3.9)
    total = row_scale * col_scale * noise + tone_field(key_tone)
    return jnp.clip(total, -40.0, 40.0).astype(jnp.bfloat16)


def block_scale(own_key, dims, shards, low, high):
    def one(dim, blocks):
        draws = jax.random.uniform(jax.random.fold_in(jax.random.fold_in(own_key, 6), dim), (blocks,), jnp.float32, low / len(shards), high / len(shards))
        return jnp.repeat(jnp.exp(draws), dims[dim] // blocks).reshape((-1,) + (1,) * (len(dims) - dim - 1))

    gain = one(*shards[0])
    for cut in shards[1:]:
        gain = gain * one(*cut)
    return gain


def bell_draw(own_key, dims, deviation, bound, pieces=(), kind=jnp.bfloat16):
    array = jax.random.normal(own_key, dims, jnp.float32) * deviation
    if len(pieces) > 0:
        array = block_scale(own_key, dims, pieces, -0.22, 0.18) * array
    return jnp.clip(array, min=-bound, max=bound).astype(kind)


def setup_inputs(seed: int = 0) -> dict:
    key_of = jax.random.split(jax.random.key(seed), 6)
    return {
        "echoes": draw_echoes(jax.random.fold_in(key_of[5], 71), 0),
        "chirp_phase": jnp.clip(jax.random.uniform(key_of[1], (PULSES,), jnp.float32, -3.140625, 3.140625), -3.140625, 3.140625),
        "sample_init": bell_draw(key_of[2], (SAMPLES, RANK), SAMPLES ** -0.5, 0.03125, ((0, 16),)),
        "threshold": jnp.clip(jax.random.uniform(key_of[3], (1,), jnp.float32, 1.0, 2.0), 1.0, 2.0),
        "ridge_scale": jnp.clip(jnp.exp(jax.random.uniform(key_of[4], (1,), jnp.float32, math.log(0.05), math.log(0.5))), 0.05, 0.5),
    }


def ridge(partial_sum, gram, ridge_scale):
    width = gram.shape[0]
    shift = ridge_scale[0] * jnp.trace(gram) / width
    system = gram + shift * jnp.eye(width, dtype=jnp.float32)
    return jnp.linalg.solve(system, partial_sum.T).T

def reference(echoes, chirp_phase, sample_init, threshold, ridge_scale):
    echo_float = echoes.astype(jnp.float32)
    sample_bf = sample_init
    sparse_part = jnp.zeros(echo_float.shape, jnp.float32)
    total_cells = PULSES * SAMPLES
    for turn_index in range(ITERS):
        cleaned = (echo_float - sparse_part).astype(jnp.bfloat16)
        pulse_partial = jnp.dot(cleaned.astype(jnp.float32), sample_bf.astype(jnp.float32), preferred_element_type=jnp.float32)
        pulse_gram = jnp.dot(sample_bf.T.astype(jnp.float32), sample_bf.astype(jnp.float32), preferred_element_type=jnp.float32)
        pulse_factor = ridge(pulse_partial, pulse_gram, ridge_scale)
        pulse_bf = pulse_factor.astype(jnp.bfloat16)
        sample_partial = jnp.dot(cleaned.T.astype(jnp.float32), pulse_bf.astype(jnp.float32), preferred_element_type=jnp.float32)
        sample_gram = jnp.dot(pulse_bf.T.astype(jnp.float32), pulse_bf.astype(jnp.float32), preferred_element_type=jnp.float32)
        sample_factor = ridge(sample_partial, sample_gram, ridge_scale)
        sample_bf = sample_factor.astype(jnp.bfloat16)
        residual = echo_float - jnp.dot(pulse_bf.astype(jnp.float32), sample_bf.T.astype(jnp.float32), preferred_element_type=jnp.float32)
        level = threshold[0] * jnp.sqrt(jnp.sum(residual * residual) / total_cells + 1e-06)
        sparse_part = residual - jnp.clip(residual, -level, level)
    clean_bf = residual.astype(jnp.bfloat16)
    bins = jnp.arange(BINS, dtype=jnp.int32) - BINS // 2
    pulses = jnp.arange(PULSES, dtype=jnp.int32)
    index = jnp.mod(bins[:, None] * pulses[None, :], PULSES).astype(jnp.int32)
    theta = 2.0 * jnp.pi * index.astype(jnp.float32) / PULSES + chirp_phase[None, :]
    scale = 1.0 / jnp.sqrt(jnp.float32(PULSES))
    kernel = (jnp.stack([jnp.cos(theta), -jnp.sin(theta)], axis=1) * scale).astype(jnp.bfloat16)
    kernel = kernel.reshape(BINS * 2, PULSES)
    doppler = jnp.dot(kernel.astype(jnp.float32), clean_bf.astype(jnp.float32), preferred_element_type=jnp.float32).reshape(BINS, 2, SAMPLES)
    return (doppler, pulse_factor, sparse_part.astype(jnp.bfloat16))
```

```python
import jax
import jax.numpy as jnp
from jax import lax
from jax.experimental import pallas as pl
from jax.experimental.pallas import tpu as pltpu
from jax.sharding import PartitionSpec as P


BINS = 256
ITERS = 2
RANK = 64
F32 = jnp.float32
BF16 = jnp.bfloat16
HIGH = lax.Precision.HIGHEST

NN = (((1,), (0,)), ((), ()))
NT = (((1,), (1,)), ((), ()))


def mm(a, b, dims):
    return lax.dot_general(a, b, dims, preferred_element_type=F32)


def mm_exact(a, b):
    return lax.dot_general(a, b, NN, precision=HIGH, preferred_element_type=F32)


def lanes_low(shape):
    return lax.broadcasted_iota(jnp.int32, shape, 1) < RANK


def pack_square(twice):
    half = RANK // 2
    return jnp.where(lanes_low((half, 128)), twice[:half], twice[half:])


def unpack_square(packed):
    swapped = pltpu.roll(packed, RANK, 1)
    low = lanes_low(packed.shape)
    return jnp.concatenate(
        [jnp.where(low, packed, swapped), jnp.where(low, swapped, packed)], axis=0
    )


def ridge_inverse(twice, ridge_scale):
    row = lax.broadcasted_iota(jnp.int32, (RANK, 128), 0)
    lane = lax.broadcasted_iota(jnp.int32, (RANK, 128), 1)
    diag = row == lane
    trace = jnp.sum(jnp.sum(jnp.where(diag, twice, 0.0), axis=0, keepdims=True), axis=1, keepdims=True)
    shift = ridge_scale * trace / RANK
    unit = (lane == row + RANK).astype(F32)
    work = jnp.where(lane < RANK, twice + jnp.where(diag, shift, 0.0), unit)
    panel = 8
    for start in range(0, RANK, panel):
        columns = [
            jnp.broadcast_to(work[:, start + j : start + j + 1], (RANK, 128)) for j in range(panel)
        ]
        for j in range(panel):
            k = start + j
            inverse = 1.0 / columns[j][k : k + 1, :]
            scaled = work[k : k + 1, :] * inverse
            for i in range(j + 1, panel):
                entry = columns[j][start + i : start + i + 1, :] * inverse
                columns[i] = jnp.where(row == k, entry, columns[i] - columns[j] * entry)
            work = jnp.where(row == k, scaled, work - columns[j] * scaled)
    swapped = pltpu.roll(work, RANK, 1)
    return jnp.where(lane < RANK, swapped, work)


def stack_factor(v_ref, va_ref, vb_ref, ta_ref=None, tb_ref=None):
    chunks, rank, width = v_ref.shape
    cols = chunks * width
    va_ref[rank:, :] = jnp.zeros((rank, cols), va_ref.dtype)
    vb_ref[:rank, :] = jnp.zeros((rank, cols), vb_ref.dtype)
    for j in range(chunks):
        part = v_ref[j]
        here = slice(j * width, (j + 1) * width)
        va_ref[:rank, here] = part
        vb_ref[rank:, here] = part
        if ta_ref is not None:
            turned = jnp.concatenate([part, part], axis=0).T
            zero = jnp.zeros_like(turned)
            low = lanes_low(turned.shape)
            ta_ref[here, :] = jnp.where(low, turned, zero)
            tb_ref[here, :] = jnp.where(low, zero, turned)


def first_products(echo_ref, v_ref, out_ref, ta, tb, gram):
    @pl.when(pl.program_id(0) == 0)
    def _():
        factor = v_ref[...]
        both = jnp.concatenate([factor, factor], axis=0)
        gram[...] = pack_square(mm(factor, both, NT))
        width = 256
        low = lanes_low((width, 128))
        zero = jnp.zeros((width, 128), BF16)
        for j in range(ta.shape[0] // width):
            here = slice(j * width, (j + 1) * width)
            turned = both[:, here].T
            ta[here, :] = jnp.where(low, turned, zero)
            tb[here, :] = jnp.where(low, zero, turned)

    part = mm(echo_ref[0], ta[...], NN) + mm(echo_ref[1], tb[...], NN)
    out_ref[:, :32, :] = part.reshape(out_ref.shape[0], 32, 128)
    out_ref[:, 32:, :] = jnp.broadcast_to(gram[...][None], (out_ref.shape[0], 32, 128))


def level_of(sums, threshold, cells):
    tile = jnp.sum(sums, axis=0)
    total = jnp.sum(jnp.sum(tile, axis=0, keepdims=True), axis=1, keepdims=True)
    return threshold * jnp.sqrt(total / cells + 1e-06)


def next_products(cells, scalars, echo_ref, u_ref, v_ref, sums_ref, out_ref, clean_ref, va, vb, ta, tb, buffer, sems):
    stack_factor(v_ref, va, vb, ta, tb)
    copies = []
    level = level_of(sums_ref[...], scalars[0:1, 0:1], cells)
    rows = u_ref.shape[0] // 2
    for i in range(2):
        here = slice(i * rows, (i + 1) * rows)
        part = None
        for h, stacked, turned in ((0, va, ta), (1, vb, tb)):
            echo = echo_ref[h, here].astype(F32)
            residual = echo - mm(u_ref[here], stacked[...], NN)
            sparse = residual - jnp.clip(residual, -level, level)
            cleaned = (echo - sparse).astype(BF16)
            buffer[h, i] = cleaned
            copy = pltpu.make_async_copy(buffer.at[h, i], clean_ref.at[h, pl.ds(i * rows, rows)], sems.at[h, i])
            copy.start()
            copies.append(copy)
            term = mm(cleaned, turned[...], NN)
            part = term if part is None else part + term
        out_ref[8 * i : 8 * (i + 1)] = part.reshape(8, 32, 128)
    for copy in copies:
        copy.wait()


def inverse_block(twice, ridge_scale):
    inverse = ridge_inverse(twice, ridge_scale)
    low = lanes_low((RANK, 128))
    return jnp.concatenate([jnp.where(low, inverse, 0.0), jnp.where(low, 0.0, inverse)], axis=0)


def invert_gram(scalars, got_ref, out_ref):
    total = jnp.sum(got_ref[:, 8:, :], axis=0)
    out_ref[...] = inverse_block(unpack_square(total), scalars[1:2, 0:1])


def solve_pulses(scalars, got_ref, out_ref):
    total = jnp.sum(got_ref[...], axis=0)
    block = inverse_block(unpack_square(total[32:]), scalars[1:2, 0:1])
    factor = mm_exact(total[:32], block).astype(out_ref.dtype)
    out_ref[...] = jnp.broadcast_to(factor[None], out_ref.shape)


def apply_pulses(got_ref, block_ref, out_ref):
    factor = mm_exact(jnp.sum(got_ref[...], axis=0), block_ref[...]).astype(out_ref.dtype)
    out_ref[...] = jnp.broadcast_to(factor[None], out_ref.shape)


def solve_samples(scalars, got_ref, out_ref, *rest):
    total = jnp.sum(got_ref[...], axis=0)
    inverse = ridge_inverse(unpack_square(total[RANK : RANK + 32]), scalars[1:2, 0:1])
    factor = mm_exact(inverse[:, :RANK], total[:RANK]).astype(out_ref.dtype)
    out_ref[...] = jnp.broadcast_to(factor[None], out_ref.shape)
    if rest:
        rest[0][...] = total[RANK + 32 :]


def sample_products(data_ref, u_ref, *refs):
    kernel_ref = refs[0] if len(refs) == 4 else None
    keep_ref, send_ref, turned = refs[-3:]
    width = 128
    own = lax.axis_index("pulse") % 2 == 0

    @pl.when(pl.program_id(0) == 0)
    def _():
        turned[...] = u_ref[...].T

    square = mm(turned[...], u_ref[...], NN)
    mixed = jnp.where(lanes_low((RANK, 128)), square[:RANK], square[RANK:])
    gram = pack_square(mixed + pltpu.roll(mixed, RANK, 1))
    product = mm(turned[:RANK], data_ref[0], NN) + mm(turned[RANK:], data_ref[1], NN)
    chunks = keep_ref.shape[0]
    for z in range(chunks):
        zero = product[:, 2 * z * width : (2 * z + 1) * width]
        one = product[:, (2 * z + 1) * width : (2 * z + 2) * width]
        keep_ref[z, :RANK, :] = jnp.where(own, zero, one)
        send_ref[z, :RANK, :] = jnp.where(own, one, zero)
        keep_ref[z, RANK : RANK + 32, :] = gram
        send_ref[z, RANK : RANK + 32, :] = gram
    if kernel_ref is not None:
        half = kernel_ref.shape[1] // 2
        low = lanes_low((kernel_ref.shape[0], 128))
        mixed = jnp.where(
            low, mm(kernel_ref[:, :half], u_ref[...], NN), mm(kernel_ref[:, half:], u_ref[...], NN)
        )
        twice = mixed + pltpu.roll(mixed, RANK, 1)
        low = lanes_low((16, 128))
        for z in range(chunks):
            mine = twice[64 * z : 64 * (z + 1)]
            zero = jnp.where(low, mine[:16], mine[16:32])
            one = jnp.where(low, mine[32:48], mine[48:])
            keep_ref[z, RANK + 32 :, :] = jnp.where(own, zero, one)
            send_ref[z, RANK + 32 :, :] = jnp.where(own, one, zero)


def residual_squares(with_gram, echo_ref, u_ref, v_ref, out_ref, va, vb):
    stack_factor(v_ref, va, vb)
    rows = u_ref.shape[0] // 2
    total = jnp.zeros((8, va.shape[1]), F32)
    for i in range(2):
        here = slice(i * rows, (i + 1) * rows)
        for h, stacked in ((0, va), (1, vb)):
            residual = echo_ref[h, here].astype(F32) - mm(u_ref[here], stacked[...], NN)
            square = residual * residual
            total = total + jnp.sum(square.reshape(-1, 8, square.shape[1]), axis=0)
    tile = total[:, :128]
    for j in range(1, total.shape[1] // 128):
        tile = tile + total[:, 128 * j : 128 * (j + 1)]
    if with_gram:
        square = mm(va[:RANK, :], va[...] + vb[...], NT)
        tile = jnp.concatenate([tile, pack_square(square)], axis=0)
    out_ref[...] = jnp.broadcast_to(tile[None], out_ref.shape)


def correct_doppler(v_ref, dop_ref, ku_ref, dop_out):
    ku = ku_ref[...]
    high = ku.astype(BF16)
    rest = ku - high.astype(F32)
    middle = rest.astype(BF16)
    low = (rest - middle.astype(F32)).astype(BF16)
    chunks, _, width = v_ref.shape
    zero = jnp.zeros((16, RANK), BF16)
    parts = []
    for part in (high, middle, low):
        parts += [part[:, :RANK], part[:, RANK:]]
    parts = jnp.concatenate(parts, axis=0)
    for j in range(chunks):
        here = slice(j * width, (j + 1) * width)
        fix = mm(parts, v_ref[j], NN)
        fix = fix[:32] + (fix[32:64] + fix[64:])
        value = dop_ref[0, :, here] - fix
        dop_out[:, 0, here] = value[:16]
        dop_out[:, 1, here] = value[16:]


def finish(cells, scalars, echo_ref, u_ref, v_ref, sums_ref, sparse_ref, va, vb, level_ref):
    @pl.when(pl.program_id(0) == 0)
    def _():
        stack_factor(v_ref, va, vb)
        level_ref[...] = jnp.broadcast_to(level_of(sums_ref[...], scalars[0:1, 0:1], cells), (1, 128))

    level = level_ref[0:1, 0:1]
    rows = echo_ref.shape[1]
    u = u_ref[pl.ds(pl.multiple_of(pl.program_id(0) * rows, rows), rows), :]
    for h, stacked in ((0, va), (1, vb)):
        residual = echo_ref[h].astype(F32) - mm(u, stacked[...], NN)
        sparse_ref[h] = (residual - jnp.clip(residual, -level, level)).astype(BF16)


def doppler_products(ca_ref, sa_ref, cb_ref, sb_ref, echo_ref, kernel_ref, out_ref):
    groups = ca_ref.shape[0]

    @pl.when(pl.program_id(0) == 0)
    def _():
        cb, sb = cb_ref[...], sb_ref[...]
        for g in range(groups):
            ca, sa = ca_ref[g : g + 1, :], sa_ref[g : g + 1, :]
            kernel_ref[32 * g : 32 * g + 16, :] = (ca * cb - sa * sb).astype(BF16)
            kernel_ref[32 * g + 16 : 32 * (g + 1), :] = (-(sa * cb + ca * sb)).astype(BF16)

    out_ref[...] = mm(kernel_ref[...], echo_ref[...], NN)


def full(shape):
    return pl.BlockSpec(shape, lambda *_: (0,) * len(shape))


VMEM = pl.BlockSpec(memory_space=pltpu.VMEM)
HBM = pl.BlockSpec(memory_space=pl.ANY)


def call(body, outs, *args, scratch=(), blocked=None, blocked_out=None, steps=None, in_hbm=()):
    blocked, blocked_out = blocked or {}, blocked_out or {}
    in_specs = [blocked.get(i, VMEM) for i in range(len(args))]
    out_specs = [blocked_out.get(i, HBM if i in in_hbm else VMEM) for i in range(len(outs))]
    shapes = [
        jax.ShapeDtypeStruct(*shape) if i in blocked_out else (pltpu.HBM if i in in_hbm else pltpu.VMEM)(*shape)
        for i, shape in enumerate(outs)
    ]
    args = [
        pltpu.with_memory_space_constraint(arg, pltpu.HBM if i in blocked else pltpu.VMEM)
        for i, arg in enumerate(args)
    ]
    return pl.pallas_call(
        body, in_specs=in_specs, out_specs=out_specs, out_shape=shapes, scratch_shapes=list(scratch),
        compiler_params=pltpu.CompilerParams(vmem_limit_bytes=28 * 2**20), **({"grid": (steps,)} if steps else {}),
    )(*args)


def on_device(echoes, chirp_phase, sample_init, threshold, ridge_scale):
    groups = lax.axis_size("pulse")
    rows, cols = echoes.shape
    half = rows // 2
    cells = rows * cols * groups * lax.axis_size("sample")
    pulse_total = rows * groups
    own_pulse = lax.axis_index("pulse")
    scalars = jnp.broadcast_to(jnp.concatenate([threshold, ridge_scale] * 4)[:, None], (8, 128))
    echo3 = echoes.reshape(2, half, cols)
    across_z = [[2 * z + c for z in range(groups // 2)] for c in range(2)]
    other_core = [(i, i ^ 1) for i in range(groups)]
    stacked = [pltpu.VMEM((128, cols), BF16)] * 2
    turned = [pltpu.VMEM((cols, 128), BF16)] * 2

    bp = half // 2
    row_blocks = pl.BlockSpec((2, bp, cols), lambda i: (0, i, 0))
    to_solve = call(
        first_products, [((16, 64, 128), F32)], echo3, sample_init.T, steps=2,
        blocked={0: row_blocks}, blocked_out={0: pl.BlockSpec((8, 64, 128), lambda i: (i, 0, 0))},
        scratch=turned + [pltpu.VMEM((32, 128), F32)],
    )[0]
    to_solve, chirp_phase = lax.optimization_barrier((to_solve, chirp_phase))
    got = lax.all_to_all(to_solve, "sample", 0, 0, tiled=True)

    pulses = own_pulse * rows + jnp.arange(rows, dtype=jnp.int32)
    phases = lax.dynamic_slice_in_dim(chirp_phase, own_pulse * rows, rows)
    steps = jnp.arange(16, dtype=jnp.int32)[:, None]
    turn = 2.0 * jnp.pi / pulse_total
    angle_a = jnp.mod((16 * steps - BINS // 2) * pulses[None, :], pulse_total).astype(F32) * turn + phases[None, :]
    angle_b = jnp.mod(steps * pulses[None, :], pulse_total).astype(F32) * turn
    scale = 1.0 / jnp.sqrt(F32(pulse_total))
    table = full((16, rows))
    dcols = 512
    kernel, spectrum = pl.pallas_call(
        doppler_products, grid=(cols // dcols,),
        in_specs=[table] * 4 + [pl.BlockSpec((rows, dcols), lambda i: (0, i))],
        out_specs=[full((2 * BINS, rows)), pl.BlockSpec((2 * BINS, dcols), lambda i: (0, i))],
        out_shape=[jax.ShapeDtypeStruct((2 * BINS, rows), BF16), jax.ShapeDtypeStruct((2 * BINS, cols), F32)],
        compiler_params=pltpu.CompilerParams(vmem_limit_bytes=56 * 2**20), name="doppler_products",
    )(jnp.cos(angle_a) * scale, jnp.sin(angle_a) * scale, jnp.cos(angle_b), jnp.sin(angle_b), echoes)
    spectrum = lax.psum_scatter(
        spectrum.reshape(groups, 2 * BINS // groups, cols), "pulse", scatter_dimension=0, tiled=True
    )

    data3 = echo3
    for turn_index in range(ITERS):
        last = turn_index == ITERS - 1
        pulse_out = [((16, 32, 128), F32 if last else BF16)]
        if turn_index == 0:
            mine = call(solve_pulses, pulse_out, scalars, got)[0]
        else:
            got = lax.all_to_all(to_solve, "sample", 0, 0, tiled=True)
            block = call(invert_gram, [((128, 128), F32)], scalars, grams)[0]
            mine = call(apply_pulses, pulse_out, got, block)[0]
        u_full = lax.all_to_all(mine, "sample", 0, 0, tiled=True).reshape(half, 128)
        u_bf = u_full.astype(BF16)
        depth = RANK + 32 + (16 if last else 0)
        extra = [kernel] if last else []
        keep, send = call(
            sample_products, [((8, depth, 128), F32)] * 2, data3, u_bf, *extra, steps=2,
            blocked={0: pl.BlockSpec((2, half, cols // 2), lambda i: (0, 0, i)), 2: pl.BlockSpec((BINS, rows), lambda i: (i, 0))},
            blocked_out={i: pl.BlockSpec((4, depth, 128), lambda i: (i, 0, 0)) for i in range(2)},
            scratch=[pltpu.VMEM((128, half), BF16)],
        )
        keep = keep + lax.ppermute(send, "pulse", other_core)
        got = lax.all_to_all(keep, "pulse", 0, 0, tiled=True, axis_index_groups=across_z)
        outs = [((16, RANK, 128), BF16)] + ([((16, 128), F32)] if last else [])
        mine = call(solve_samples, outs, scalars, got)
        v_chunks = lax.all_to_all(mine[0], "pulse", 0, 0, tiled=True)
        height = 8 if last else 40
        grams = call(
            lambda *refs: residual_squares(not last, *refs), [((16, height, 128), F32)],
            echo3, u_bf, v_chunks, scratch=stacked,
        )[0]
        grams = lax.all_to_all(grams, "sample", 0, 0, tiled=True)
        sums = jnp.sum(grams[:, :8], axis=0, keepdims=True)
        if last:
            sums, spectrum = lax.optimization_barrier((sums, spectrum))
        sums = lax.all_to_all(jnp.broadcast_to(sums, (16, 8, 128)), "pulse", 0, 0, tiled=True)
        if not last:
            to_solve, data3 = call(
                lambda *refs: next_products(cells, *refs),
                [((16, 32, 128), F32), (echo3.shape, BF16)],
                scalars, echo3, u_bf, v_chunks, sums, in_hbm=(1,),
                scratch=stacked + turned + [pltpu.VMEM((2, 2, bp, cols), BF16), pltpu.SemaphoreType.DMA((2, 2))],
            )
    doppler = call(correct_doppler, [((16, 2, cols), F32)], v_chunks, spectrum, mine[1])[0]
    sums, doppler = lax.optimization_barrier((sums, doppler))
    sparse = call(
        lambda *refs: finish(cells, *refs), [(echo3.shape, BF16)],
        scalars, echo3, u_bf, v_chunks, sums, steps=2, blocked={1: row_blocks}, blocked_out={0: row_blocks},
        scratch=stacked + [pltpu.VMEM((1, 128), F32)],
    )[0]
    turned_factor = u_full.T
    pulse_factor = jnp.concatenate([turned_factor[:RANK], turned_factor[RANK:]], axis=1).T
    return (doppler, pulse_factor, sparse.reshape(rows, cols))


def solution(mesh):
    placed = (P("pulse", "sample"), P(), P("sample", None), P(), P())
    return jax.shard_map(
        on_device,
        mesh=mesh,
        in_specs=placed,
        out_specs=(P("pulse", None, "sample"), P("pulse", None), P("pulse", "sample")),
        check_vma=False,
    )
```

```python
import jax
import jax.numpy as jnp
from jax import lax
from jax.experimental import pallas as pl
from jax.experimental.pallas import tpu as pltpu
from jax.sharding import PartitionSpec as P


BINS = 256
ITERS = 2
RANK = 64
F32 = jnp.float32
BF16 = jnp.bfloat16
HIGH = lax.Precision.HIGHEST

NN = (((1,), (0,)), ((), ()))
NT = (((1,), (1,)), ((), ()))


def mm(a, b, dims):
    return lax.dot_general(a, b, dims, preferred_element_type=F32)


def mm_exact(a, b):
    return lax.dot_general(a, b, NN, precision=HIGH, preferred_element_type=F32)


def lanes_low(shape):
    return lax.broadcasted_iota(jnp.int32, shape, 1) < RANK


def pack_square(twice):
    half = RANK // 2
    return jnp.where(lanes_low((half, 128)), twice[:half], twice[half:])


def unpack_square(packed):
    swapped = pltpu.roll(packed, RANK, 1)
    low = lanes_low(packed.shape)
    return jnp.concatenate(
        [jnp.where(low, packed, swapped), jnp.where(low, swapped, packed)], axis=0
    )


def ridge_inverse(twice, ridge_scale):
    row = lax.broadcasted_iota(jnp.int32, (RANK, 128), 0)
    lane = lax.broadcasted_iota(jnp.int32, (RANK, 128), 1)
    diag = row == lane
    trace = jnp.sum(jnp.sum(jnp.where(diag, twice, 0.0), axis=0, keepdims=True), axis=1, keepdims=True)
    shift = ridge_scale * trace / RANK
    unit = (lane == row + RANK).astype(F32)
    work = jnp.where(lane < RANK, twice + jnp.where(diag, shift, 0.0), unit)
    panel = 8
    for start in range(0, RANK, panel):
        columns = [
            jnp.broadcast_to(work[:, start + j : start + j + 1], (RANK, 128)) for j in range(panel)
        ]
        for j in range(panel):
            k = start + j
            inverse = 1.0 / columns[j][k : k + 1, :]
            scaled = work[k : k + 1, :] * inverse
            for i in range(j + 1, panel):
                entry = columns[j][start + i : start + i + 1, :] * inverse
                columns[i] = jnp.where(row == k, entry, columns[i] - columns[j] * entry)
            work = jnp.where(row == k, scaled, work - columns[j] * scaled)
    swapped = pltpu.roll(work, RANK, 1)
    return jnp.where(lane < RANK, swapped, work)


def stack_factor(v_ref, va_ref, vb_ref, ta_ref=None, tb_ref=None):
    chunks, rank, width = v_ref.shape
    cols = chunks * width
    va_ref[rank:, :] = jnp.zeros((rank, cols), va_ref.dtype)
    vb_ref[:rank, :] = jnp.zeros((rank, cols), vb_ref.dtype)
    for j in range(chunks):
        part = v_ref[j]
        here = slice(j * width, (j + 1) * width)
        va_ref[:rank, here] = part
        vb_ref[rank:, here] = part
        if ta_ref is not None:
            turned = jnp.concatenate([part, part], axis=0).T
            zero = jnp.zeros_like(turned)
            low = lanes_low(turned.shape)
            ta_ref[here, :] = jnp.where(low, turned, zero)
            tb_ref[here, :] = jnp.where(low, zero, turned)


def first_products(echo_ref, v_ref, out_ref, ta, tb, gram):
    @pl.when(pl.program_id(0) == 0)
    def _():
        factor = v_ref[...]
        both = jnp.concatenate([factor, factor], axis=0)
        gram[...] = pack_square(mm(factor, both, NT))
        width = 256
        low = lanes_low((width, 128))
        zero = jnp.zeros((width, 128), BF16)
        for j in range(ta.shape[0] // width):
            here = slice(j * width, (j + 1) * width)
            turned = both[:, here].T
            ta[here, :] = jnp.where(low, turned, zero)
            tb[here, :] = jnp.where(low, zero, turned)

    part = mm(echo_ref[0], ta[...], NN) + mm(echo_ref[1], tb[...], NN)
    out_ref[:, :32, :] = part.reshape(out_ref.shape[0], 32, 128)
    out_ref[:, 32:, :] = jnp.broadcast_to(gram[...][None], (out_ref.shape[0], 32, 128))


def level_of(sums, threshold, cells):
    tile = jnp.sum(sums, axis=0)
    total = jnp.sum(jnp.sum(tile, axis=0, keepdims=True), axis=1, keepdims=True)
    return threshold * jnp.sqrt(total / cells + 1e-06)


def next_products(cells, scalars, echo_ref, u_ref, v_ref, sums_ref, out_ref, clean_ref, va, vb, ta, tb, buffer, sems):
    stack_factor(v_ref, va, vb, ta, tb)
    copies = []
    level = level_of(sums_ref[...], scalars[0:1, 0:1], cells)
    rows = u_ref.shape[0] // 2
    for i in range(2):
        here = slice(i * rows, (i + 1) * rows)
        part = None
        for h, stacked, turned in ((0, va, ta), (1, vb, tb)):
            echo = echo_ref[h, here].astype(F32)
            residual = echo - mm(u_ref[here], stacked[...], NN)
            sparse = residual - jnp.clip(residual, -level, level)
            cleaned = (echo - sparse).astype(BF16)
            buffer[h, i] = cleaned
            copy = pltpu.make_async_copy(buffer.at[h, i], clean_ref.at[h, pl.ds(i * rows, rows)], sems.at[h, i])
            copy.start()
            copies.append(copy)
            term = mm(cleaned, turned[...], NN)
            part = term if part is None else part + term
        out_ref[8 * i : 8 * (i + 1)] = part.reshape(8, 32, 128)
    for copy in copies:
        copy.wait()


def inverse_block(twice, ridge_scale):
    inverse = ridge_inverse(twice, ridge_scale)
    low = lanes_low((RANK, 128))
    return jnp.concatenate([jnp.where(low, inverse, 0.0), jnp.where(low, 0.0, inverse)], axis=0)


def invert_gram(scalars, got_ref, out_ref):
    total = jnp.sum(got_ref[:, 8:, :], axis=0)
    out_ref[...] = inverse_block(unpack_square(total), scalars[1:2, 0:1])


def solve_pulses(scalars, got_ref, out_ref):
    total = jnp.sum(got_ref[...], axis=0)
    block = inverse_block(unpack_square(total[32:]), scalars[1:2, 0:1])
    factor = mm_exact(total[:32], block).astype(out_ref.dtype)
    out_ref[...] = jnp.broadcast_to(factor[None], out_ref.shape)


def apply_pulses(got_ref, block_ref, out_ref):
    factor = mm_exact(jnp.sum(got_ref[...], axis=0), block_ref[...]).astype(out_ref.dtype)
    out_ref[...] = jnp.broadcast_to(factor[None], out_ref.shape)


def solve_samples(scalars, got_ref, out_ref, *rest):
    total = jnp.sum(got_ref[...], axis=0)
    inverse = ridge_inverse(unpack_square(total[RANK : RANK + 32]), scalars[1:2, 0:1])
    factor = mm_exact(inverse[:, :RANK], total[:RANK]).astype(out_ref.dtype)
    out_ref[...] = jnp.broadcast_to(factor[None], out_ref.shape)
    if rest:
        rest[0][...] = total[RANK + 32 :]


def sample_products(data_ref, u_ref, *refs):
    kernel_ref = refs[0] if len(refs) == 4 else None
    keep_ref, send_ref, turned = refs[-3:]
    width = 128
    own = lax.axis_index("pulse") % 2 == 0

    @pl.when(pl.program_id(0) == 0)
    def _():
        turned[...] = u_ref[...].T

    square = mm(turned[...], u_ref[...], NN)
    mixed = jnp.where(lanes_low((RANK, 128)), square[:RANK], square[RANK:])
    gram = pack_square(mixed + pltpu.roll(mixed, RANK, 1))
    product = mm(turned[:RANK], data_ref[0], NN) + mm(turned[RANK:], data_ref[1], NN)
    chunks = keep_ref.shape[0]
    for z in range(chunks):
        zero = product[:, 2 * z * width : (2 * z + 1) * width]
        one = product[:, (2 * z + 1) * width : (2 * z + 2) * width]
        keep_ref[z, :RANK, :] = jnp.where(own, zero, one)
        send_ref[z, :RANK, :] = jnp.where(own, one, zero)
        keep_ref[z, RANK : RANK + 32, :] = gram
        send_ref[z, RANK : RANK + 32, :] = gram
    if kernel_ref is not None:
        half = kernel_ref.shape[1] // 2
        low = lanes_low((kernel_ref.shape[0], 128))
        mixed = jnp.where(
            low, mm(kernel_ref[:, :half], u_ref[...], NN), mm(kernel_ref[:, half:], u_ref[...], NN)
        )
        twice = mixed + pltpu.roll(mixed, RANK, 1)
        low = lanes_low((16, 128))
        for z in range(chunks):
            mine = twice[64 * z : 64 * (z + 1)]
            zero = jnp.where(low, mine[:16], mine[16:32])
            one = jnp.where(low, mine[32:48], mine[48:])
            keep_ref[z, RANK + 32 :, :] = jnp.where(own, zero, one)
            send_ref[z, RANK + 32 :, :] = jnp.where(own, one, zero)


def residual_squares(with_gram, echo_ref, u_ref, v_ref, out_ref, va, vb):
    stack_factor(v_ref, va, vb)
    rows = u_ref.shape[0] // 2
    total = jnp.zeros((8, va.shape[1]), F32)
    for i in range(2):
        here = slice(i * rows, (i + 1) * rows)
        for h, stacked in ((0, va), (1, vb)):
            residual = echo_ref[h, here].astype(F32) - mm(u_ref[here], stacked[...], NN)
            square = residual * residual
            total = total + jnp.sum(square.reshape(-1, 8, square.shape[1]), axis=0)
    tile = total[:, :128]
    for j in range(1, total.shape[1] // 128):
        tile = tile + total[:, 128 * j : 128 * (j + 1)]
    if with_gram:
        square = mm(va[:RANK, :], va[...] + vb[...], NT)
        tile = jnp.concatenate([tile, pack_square(square)], axis=0)
    out_ref[...] = jnp.broadcast_to(tile[None], out_ref.shape)


def correct_doppler(v_ref, dop_ref, ku_ref, dop_out):
    ku = ku_ref[...]
    high = ku.astype(BF16)
    rest = ku - high.astype(F32)
    middle = rest.astype(BF16)
    low = (rest - middle.astype(F32)).astype(BF16)
    chunks, _, width = v_ref.shape
    zero = jnp.zeros((16, RANK), BF16)
    parts = []
    for part in (high, middle, low):
        parts += [part[:, :RANK], part[:, RANK:]]
    parts = jnp.concatenate(parts, axis=0)
    for j in range(chunks):
        here = slice(j * width, (j + 1) * width)
        fix = mm(parts, v_ref[j], NN)
        fix = fix[:32] + (fix[32:64] + fix[64:])
        value = dop_ref[0, :, here] - fix
        dop_out[:, 0, here] = value[:16]
        dop_out[:, 1, here] = value[16:]


def finish(cells, scalars, echo_ref, u_ref, v_ref, sums_ref, sparse_ref, va, vb, level_ref):
    @pl.when(pl.program_id(0) == 0)
    def _():
        stack_factor(v_ref, va, vb)
        level_ref[...] = jnp.broadcast_to(level_of(sums_ref[...], scalars[0:1, 0:1], cells), (1, 128))

    level = level_ref[0:1, 0:1]
    rows = echo_ref.shape[1]
    u = u_ref[pl.ds(pl.multiple_of(pl.program_id(0) * rows, rows), rows), :]
    for h, stacked in ((0, va), (1, vb)):
        residual = echo_ref[h].astype(F32) - mm(u, stacked[...], NN)
        sparse_ref[h] = (residual - jnp.clip(residual, -level, level)).astype(BF16)


def doppler_products(ca_ref, sa_ref, cb_ref, sb_ref, echo_ref, kernel_ref, out_ref):
    groups = ca_ref.shape[0]

    @pl.when(pl.program_id(0) == 0)
    def _():
        cb, sb = cb_ref[...], sb_ref[...]
        for g in range(groups):
            ca, sa = ca_ref[g : g + 1, :], sa_ref[g : g + 1, :]
            kernel_ref[32 * g : 32 * g + 16, :] = (ca * cb - sa * sb).astype(BF16)
            kernel_ref[32 * g + 16 : 32 * (g + 1), :] = (-(sa * cb + ca * sb)).astype(BF16)

    out_ref[...] = mm(kernel_ref[...], echo_ref[...], NN)


def full(shape):
    return pl.BlockSpec(shape, lambda *_: (0,) * len(shape))


VMEM = pl.BlockSpec(memory_space=pltpu.VMEM)
HBM = pl.BlockSpec(memory_space=pl.ANY)


def call(body, outs, *args, scratch=(), blocked=None, blocked_out=None, steps=None, in_hbm=()):
    blocked, blocked_out = blocked or {}, blocked_out or {}
    in_specs = [blocked.get(i, VMEM) for i in range(len(args))]
    out_specs = [blocked_out.get(i, HBM if i in in_hbm else VMEM) for i in range(len(outs))]
    shapes = [
        jax.ShapeDtypeStruct(*shape) if i in blocked_out else (pltpu.HBM if i in in_hbm else pltpu.VMEM)(*shape)
        for i, shape in enumerate(outs)
    ]
    args = [
        pltpu.with_memory_space_constraint(arg, pltpu.HBM if i in blocked else pltpu.VMEM)
        for i, arg in enumerate(args)
    ]
    return pl.pallas_call(
        body, in_specs=in_specs, out_specs=out_specs, out_shape=shapes, scratch_shapes=list(scratch),
        compiler_params=pltpu.CompilerParams(vmem_limit_bytes=28 * 2**20), **({"grid": (steps,)} if steps else {}),
    )(*args)


def on_device(echoes, chirp_phase, sample_init, threshold, ridge_scale):
    groups = lax.axis_size("pulse")
    rows, cols = echoes.shape
    half = rows // 2
    cells = rows * cols * groups * lax.axis_size("sample")
    pulse_total = rows * groups
    own_pulse = lax.axis_index("pulse")
    scalars = jnp.broadcast_to(jnp.concatenate([threshold, ridge_scale] * 4)[:, None], (8, 128))
    echo3 = echoes.reshape(2, half, cols)
    across_z = [[2 * z + c for z in range(groups // 2)] for c in range(2)]
    other_core = [(i, i ^ 1) for i in range(groups)]
    stacked = [pltpu.VMEM((128, cols), BF16)] * 2
    turned = [pltpu.VMEM((cols, 128), BF16)] * 2

    bp = half // 2
    row_blocks = pl.BlockSpec((2, bp, cols), lambda i: (0, i, 0))
    to_solve = call(
        first_products, [((16, 64, 128), F32)], echo3, sample_init.T, steps=2,
        blocked={0: row_blocks, 1: full((RANK, cols))},
        blocked_out={0: pl.BlockSpec((8, 64, 128), lambda i: (i, 0, 0))},
        scratch=turned + [pltpu.VMEM((32, 128), F32)],
    )[0]
    to_solve, chirp_phase = lax.optimization_barrier((to_solve, chirp_phase))
    got = lax.all_to_all(to_solve, "sample", 0, 0, tiled=True)

    pulses = own_pulse * rows + jnp.arange(rows, dtype=jnp.int32)
    phases = lax.dynamic_slice_in_dim(chirp_phase, own_pulse * rows, rows)
    steps = jnp.arange(16, dtype=jnp.int32)[:, None]
    turn = 2.0 * jnp.pi / pulse_total
    angle_a = jnp.mod((16 * steps - BINS // 2) * pulses[None, :], pulse_total).astype(F32) * turn + phases[None, :]
    angle_b = jnp.mod(steps * pulses[None, :], pulse_total).astype(F32) * turn
    scale = 1.0 / jnp.sqrt(F32(pulse_total))
    table = full((16, rows))
    dcols = 512
    kernel, spectrum = pl.pallas_call(
        doppler_products, grid=(cols // dcols,),
        in_specs=[table] * 4 + [pl.BlockSpec((rows, dcols), lambda i: (0, i))],
        out_specs=[full((2 * BINS, rows)), pl.BlockSpec((2 * BINS, dcols), lambda i: (0, i))],
        out_shape=[jax.ShapeDtypeStruct((2 * BINS, rows), BF16), jax.ShapeDtypeStruct((2 * BINS, cols), F32)],
        compiler_params=pltpu.CompilerParams(vmem_limit_bytes=56 * 2**20), name="doppler_products",
    )(jnp.cos(angle_a) * scale, jnp.sin(angle_a) * scale, jnp.cos(angle_b), jnp.sin(angle_b), echoes)

    data3 = echo3
    for turn_index in range(ITERS):
        last = turn_index == ITERS - 1
        pulse_out = [((16, 32, 128), F32 if last else BF16)]
        if turn_index == 0:
            mine = call(solve_pulses, pulse_out, scalars, got)[0]
        else:
            got = lax.all_to_all(to_solve, "sample", 0, 0, tiled=True)
            block = call(invert_gram, [((128, 128), F32)], scalars, grams)[0]
            mine = call(apply_pulses, pulse_out, got, block)[0]
        u_full = lax.all_to_all(mine, "sample", 0, 0, tiled=True).reshape(half, 128)
        u_bf = u_full.astype(BF16)
        depth = RANK + 32 + (16 if last else 0)
        extra = [kernel] if last else []
        keep, send = call(
            sample_products, [((8, depth, 128), F32)] * 2, data3, u_bf, *extra, steps=2,
            blocked={0: pl.BlockSpec((2, half, cols // 2), lambda i: (0, 0, i)), 2: pl.BlockSpec((BINS, rows), lambda i: (i, 0))},
            blocked_out={i: pl.BlockSpec((4, depth, 128), lambda i: (i, 0, 0)) for i in range(2)},
            scratch=[pltpu.VMEM((128, half), BF16)],
        )
        keep = keep + lax.ppermute(send, "pulse", other_core)
        got = lax.all_to_all(keep, "pulse", 0, 0, tiled=True, axis_index_groups=across_z)
        outs = [((16, RANK, 128), BF16)] + ([((16, 128), F32)] if last else [])
        mine = call(solve_samples, outs, scalars, got)
        v_chunks = lax.all_to_all(mine[0], "pulse", 0, 0, tiled=True)
        height = 8 if last else 40
        grams = call(
            lambda *refs: residual_squares(not last, *refs), [((16, height, 128), F32)],
            echo3, u_bf, v_chunks, scratch=stacked,
        )[0]
        if not last:
            grams, spectrum = lax.optimization_barrier((grams, spectrum))
            spectrum = lax.psum_scatter(
                spectrum.reshape(groups, 2 * BINS // groups, cols), "pulse", scatter_dimension=0, tiled=True
            )
        grams = lax.all_to_all(grams, "sample", 0, 0, tiled=True)
        sums = jnp.sum(grams[:, :8], axis=0, keepdims=True)
        if last:
            sums, spectrum = lax.optimization_barrier((sums, spectrum))
        sums = lax.all_to_all(jnp.broadcast_to(sums, (16, 8, 128)), "pulse", 0, 0, tiled=True)
        if not last:
            to_solve, data3 = call(
                lambda *refs: next_products(cells, *refs),
                [((16, 32, 128), F32), (echo3.shape, BF16)],
                scalars, echo3, u_bf, v_chunks, sums, in_hbm=(1,),
                scratch=stacked + turned + [pltpu.VMEM((2, 2, bp, cols), BF16), pltpu.SemaphoreType.DMA((2, 2))],
            )
    doppler = call(correct_doppler, [((16, 2, cols), F32)], v_chunks, spectrum, mine[1])[0]
    sums, doppler = lax.optimization_barrier((sums, doppler))
    sparse = call(
        lambda *refs: finish(cells, *refs), [(echo3.shape, BF16)],
        scalars, echo3, u_bf, v_chunks, sums, steps=2, blocked={1: row_blocks}, blocked_out={0: row_blocks},
        scratch=stacked + [pltpu.VMEM((1, 128), F32)],
    )[0]
    turned_factor = u_full.T
    pulse_factor = jnp.concatenate([turned_factor[:RANK], turned_factor[RANK:]], axis=1).T
    return (doppler, pulse_factor, sparse.reshape(rows, cols))


def solution(mesh):
    placed = (P("pulse", "sample"), P(), P("sample", None), P(), P())
    return jax.shard_map(
        on_device,
        mesh=mesh,
        in_specs=placed,
        out_specs=(P("pulse", None, "sample"), P("pulse", None), P("pulse", "sample")),
        check_vma=False,
    )
```

```python
import jax
import jax.numpy as jnp
from jax import lax
from jax.experimental import pallas as pl
from jax.experimental.pallas import tpu as pltpu
from jax.sharding import PartitionSpec as P


BINS = 256
ITERS = 2
FALLBACK = True
RANK = 64
F32 = jnp.float32
BF16 = jnp.bfloat16
HIGH = lax.Precision.HIGHEST

NN = (((1,), (0,)), ((), ()))
NT = (((1,), (1,)), ((), ()))


def mm(a, b, dims):
    return lax.dot_general(a, b, dims, preferred_element_type=F32)


def mm_exact(a, b):
    return lax.dot_general(a, b, NN, precision=HIGH, preferred_element_type=F32)


def lanes_low(shape):
    return lax.broadcasted_iota(jnp.int32, shape, 1) < RANK


def pack_square(twice):
    half = RANK // 2
    return jnp.where(lanes_low((half, 128)), twice[:half], twice[half:])


def unpack_square(packed):
    swapped = pltpu.roll(packed, RANK, 1)
    low = lanes_low(packed.shape)
    return jnp.concatenate(
        [jnp.where(low, packed, swapped), jnp.where(low, swapped, packed)], axis=0
    )


def ridge_inverse(twice, ridge_scale):
    row = lax.broadcasted_iota(jnp.int32, (RANK, 128), 0)
    lane = lax.broadcasted_iota(jnp.int32, (RANK, 128), 1)
    diag = row == lane
    trace = jnp.sum(jnp.sum(jnp.where(diag, twice, 0.0), axis=0, keepdims=True), axis=1, keepdims=True)
    shift = ridge_scale * trace / RANK
    unit = (lane == row + RANK).astype(F32)
    work = jnp.where(lane < RANK, twice + jnp.where(diag, shift, 0.0), unit)
    panel = 8
    for start in range(0, RANK, panel):
        columns = [
            jnp.broadcast_to(work[:, start + j : start + j + 1], (RANK, 128)) for j in range(panel)
        ]
        for j in range(panel):
            k = start + j
            inverse = 1.0 / columns[j][k : k + 1, :]
            scaled = work[k : k + 1, :] * inverse
            for i in range(j + 1, panel):
                entry = columns[j][start + i : start + i + 1, :] * inverse
                columns[i] = jnp.where(row == k, entry, columns[i] - columns[j] * entry)
            work = jnp.where(row == k, scaled, work - columns[j] * scaled)
    swapped = pltpu.roll(work, RANK, 1)
    return jnp.where(lane < RANK, swapped, work)


def stack_factor(v_ref, va_ref, vb_ref, ta_ref=None, tb_ref=None):
    chunks, _, width = v_ref.shape
    rank = RANK
    cols = chunks * width
    va_ref[rank:, :] = jnp.zeros((rank, cols), va_ref.dtype)
    vb_ref[:rank, :] = jnp.zeros((rank, cols), vb_ref.dtype)
    for j in range(chunks):
        part = v_ref[j, :rank]
        here = slice(j * width, (j + 1) * width)
        va_ref[:rank, here] = part
        vb_ref[rank:, here] = part
        if ta_ref is not None:
            turned = jnp.concatenate([part, part], axis=0).T
            zero = jnp.zeros_like(turned)
            low = lanes_low(turned.shape)
            ta_ref[here, :] = jnp.where(low, turned, zero)
            tb_ref[here, :] = jnp.where(low, zero, turned)


def first_products(echo_ref, v_ref, out_ref, ta, tb, gram):
    @pl.when(pl.program_id(0) == 0)
    def _():
        factor = v_ref[...]
        both = jnp.concatenate([factor, factor], axis=0)
        gram[...] = pack_square(mm(factor, both, NT))
        width = 256
        low = lanes_low((width, 128))
        zero = jnp.zeros((width, 128), BF16)
        for j in range(ta.shape[0] // width):
            here = slice(j * width, (j + 1) * width)
            turned = both[:, here].T
            ta[here, :] = jnp.where(low, turned, zero)
            tb[here, :] = jnp.where(low, zero, turned)

    part = mm(echo_ref[0], ta[...], NN) + mm(echo_ref[1], tb[...], NN)
    out_ref[:, :32, :] = part.reshape(out_ref.shape[0], 32, 128)
    out_ref[:, 32:, :] = jnp.broadcast_to(gram[...][None], (out_ref.shape[0], 32, 128))


def total_of(tile):
    return jnp.sum(jnp.sum(tile, axis=0, keepdims=True), axis=1, keepdims=True)


def level_of(sums, threshold, cells):
    return threshold * jnp.sqrt(total_of(sums) / cells + 1e-06)


def next_products(cells, scalars, echo_ref, u_ref, v_ref, sums_ref, out_ref, clean_ref, va, vb, ta, tb, buffer, sems):
    stack_factor(v_ref, va, vb, ta, tb)
    copies = []
    level = level_of(sums_ref[...], scalars[0:1, 0:1], cells)
    rows = u_ref.shape[0] // 2
    for i in range(2):
        here = slice(i * rows, (i + 1) * rows)
        part = None
        for h, stacked, turned in ((0, va, ta), (1, vb, tb)):
            echo = echo_ref[h, here].astype(F32)
            residual = echo - mm(u_ref[here], stacked[...], NN)
            sparse = residual - jnp.clip(residual, -level, level)
            cleaned = (echo - sparse).astype(BF16)
            buffer[h, i] = cleaned
            copy = pltpu.make_async_copy(buffer.at[h, i], clean_ref.at[h, pl.ds(i * rows, rows)], sems.at[h, i])
            copy.start()
            copies.append(copy)
            term = mm(cleaned, turned[...], NN)
            part = term if part is None else part + term
        out_ref[8 * i : 8 * (i + 1)] = part.reshape(8, 32, 128)
    for copy in copies:
        copy.wait()


def inverse_block(twice, ridge_scale):
    inverse = ridge_inverse(twice, ridge_scale)
    low = lanes_low((RANK, 128))
    return jnp.concatenate([jnp.where(low, inverse, 0.0), jnp.where(low, 0.0, inverse)], axis=0)


def invert_gram(scalars, got_ref, out_ref):
    total = jnp.sum(got_ref[:, 16:, :], axis=0)
    out_ref[...] = inverse_block(unpack_square(total), scalars[1:2, 0:1])


def solve_pulses(scalars, got_ref, out_ref):
    total = jnp.sum(got_ref[...], axis=0)
    block = inverse_block(unpack_square(total[32:]), scalars[1:2, 0:1])
    factor = mm_exact(total[:32], block).astype(out_ref.dtype)
    out_ref[...] = jnp.broadcast_to(factor[None], out_ref.shape)


def apply_pulses(got_ref, block_ref, out_ref):
    factor = mm_exact(jnp.sum(got_ref[...], axis=0), block_ref[...]).astype(out_ref.dtype)
    out_ref[...] = jnp.broadcast_to(factor[None], out_ref.shape)


def solve_samples(scalars, got_ref, out_ref, rest_ref):
    total = jnp.sum(got_ref[...], axis=0)
    inverse = ridge_inverse(unpack_square(total[RANK : RANK + 32]), scalars[1:2, 0:1])
    factor = mm_exact(inverse[:, :RANK], total[:RANK]).astype(out_ref.dtype)
    if out_ref.shape[1] > RANK:
        inner = total_of(total[:RANK] * factor.astype(F32))
        high = inner.astype(BF16).astype(F32)
        middle = (inner - high).astype(BF16).astype(F32)
        low = inner - high - middle
        row = lax.broadcasted_iota(jnp.int32, (16, 128), 0)
        tail = jnp.where(row == 0, high, jnp.where(row == 1, middle, jnp.where(row == 2, low, 0.0)))
        factor = jnp.concatenate([factor, tail.astype(out_ref.dtype)], axis=0)
        rest_ref[...] = total[RANK:]
    else:
        rest_ref[...] = total[RANK + 32 :]
    out_ref[...] = jnp.broadcast_to(factor[None], out_ref.shape)


def sample_gram(v_ref, rest_ref, out_ref):
    chunks = v_ref.shape[0]
    square = jnp.zeros((RANK, 128), F32)
    inner = jnp.zeros((1, 1), F32)
    for j in range(chunks):
        part = v_ref[j, :RANK]
        square = square + mm(part, jnp.concatenate([part, part], axis=0), NT)
        tail = v_ref[j, RANK:].astype(F32)
        inner = inner + (tail[0:1, 0:1] + (tail[1:2, 0:1] + tail[2:3, 0:1]))
    tile = jnp.concatenate(
        [rest_ref[32:], jnp.broadcast_to(inner, (8, 128)), pack_square(square)], axis=0
    )
    out_ref[...] = jnp.broadcast_to(tile[None], out_ref.shape)


def squares_from_products(got_ref, rest_ref, sums_ref, energy_ref):
    total = jnp.sum(got_ref[...], axis=0)
    energy = total_of(total[:8])
    value = energy - 2.0 * total[8:9, 0:1] + total_of(total[16:] * rest_ref[:32])
    row = lax.broadcasted_iota(jnp.int32, (8, 128), 0)
    lane = lax.broadcasted_iota(jnp.int32, (8, 128), 1)
    sums_ref[...] = jnp.where((row == 0) & (lane == 0), value, 0.0)
    energy_ref[...] = jnp.broadcast_to(energy, (8, 128))


def sample_products(data_ref, u_ref, *refs):
    extra_ref = refs[0]
    kernel_ref = extra_ref if extra_ref.dtype == BF16 else None
    keep_ref, send_ref, turned = refs[-3:]
    width = 128
    own = lax.axis_index("pulse") % 2 == 0

    @pl.when(pl.program_id(0) == 0)
    def _():
        turned[...] = u_ref[...].T

    square = mm(turned[...], u_ref[...], NN)
    mixed = jnp.where(lanes_low((RANK, 128)), square[:RANK], square[RANK:])
    gram = pack_square(mixed + pltpu.roll(mixed, RANK, 1))
    product = mm(turned[:RANK], data_ref[0], NN) + mm(turned[RANK:], data_ref[1], NN)
    chunks = keep_ref.shape[0]
    for z in range(chunks):
        zero = product[:, 2 * z * width : (2 * z + 1) * width]
        one = product[:, (2 * z + 1) * width : (2 * z + 2) * width]
        keep_ref[z, :RANK, :] = jnp.where(own, zero, one)
        send_ref[z, :RANK, :] = jnp.where(own, one, zero)
        keep_ref[z, RANK : RANK + 32, :] = gram
        send_ref[z, RANK : RANK + 32, :] = gram
    if kernel_ref is None:
        energy = jnp.broadcast_to(extra_ref[...][None], (chunks, 8, 128))
        keep_ref[:, RANK + 32 :, :] = energy
        send_ref[:, RANK + 32 :, :] = energy
    else:
        half = kernel_ref.shape[1] // 2
        low = lanes_low((kernel_ref.shape[0], 128))
        mixed = jnp.where(
            low, mm(kernel_ref[:, :half], u_ref[...], NN), mm(kernel_ref[:, half:], u_ref[...], NN)
        )
        twice = mixed + pltpu.roll(mixed, RANK, 1)
        low = lanes_low((16, 128))
        for z in range(chunks):
            mine = twice[64 * z : 64 * (z + 1)]
            zero = jnp.where(low, mine[:16], mine[16:32])
            one = jnp.where(low, mine[32:48], mine[48:])
            keep_ref[z, RANK + 32 :, :] = jnp.where(own, zero, one)
            send_ref[z, RANK + 32 :, :] = jnp.where(own, one, zero)


def residual_squares(echo_ref, u_ref, v_ref, out_ref, va, vb):
    stack_factor(v_ref, va, vb)
    rows = u_ref.shape[0] // 2
    total = jnp.zeros((8, va.shape[1]), F32)
    for i in range(2):
        here = slice(i * rows, (i + 1) * rows)
        for h, stacked in ((0, va), (1, vb)):
            residual = echo_ref[h, here].astype(F32) - mm(u_ref[here], stacked[...], NN)
            square = residual * residual
            total = total + jnp.sum(square.reshape(-1, 8, square.shape[1]), axis=0)
    tile = total[:, :128]
    for j in range(1, total.shape[1] // 128):
        tile = tile + total[:, 128 * j : 128 * (j + 1)]
    out_ref[...] = jnp.broadcast_to(tile[None], out_ref.shape)


def correct_doppler(v_ref, dop_ref, ku_ref, dop_out):
    ku = ku_ref[...]
    high = ku.astype(BF16)
    rest = ku - high.astype(F32)
    middle = rest.astype(BF16)
    low = (rest - middle.astype(F32)).astype(BF16)
    chunks, _, width = v_ref.shape
    zero = jnp.zeros((16, RANK), BF16)
    parts = []
    for part in (high, middle, low):
        parts += [part[:, :RANK], part[:, RANK:]]
    parts = jnp.concatenate(parts, axis=0)
    for j in range(chunks):
        here = slice(j * width, (j + 1) * width)
        fix = mm(parts, v_ref[j], NN)
        fix = fix[:32] + (fix[32:64] + fix[64:])
        value = dop_ref[0, :, here] - fix
        dop_out[:, 0, here] = value[:16]
        dop_out[:, 1, here] = value[16:]


def finish(cells, scalars, echo_ref, u_ref, v_ref, sums_ref, sparse_ref, va, vb, level_ref):
    @pl.when(pl.program_id(0) == 0)
    def _():
        stack_factor(v_ref, va, vb)
        level_ref[...] = jnp.broadcast_to(level_of(sums_ref[...], scalars[0:1, 0:1], cells), (1, 128))

    level = level_ref[0:1, 0:1]
    rows = echo_ref.shape[1]
    u = u_ref[pl.ds(pl.multiple_of(pl.program_id(0) * rows, rows), rows), :]
    for h, stacked in ((0, va), (1, vb)):
        residual = echo_ref[h].astype(F32) - mm(u, stacked[...], NN)
        sparse_ref[h] = (residual - jnp.clip(residual, -level, level)).astype(BF16)


def doppler_products(ca_ref, sa_ref, cb_ref, sb_ref, echo_ref, kernel_ref, out_ref, energy_ref):
    groups = ca_ref.shape[0]

    @pl.when(pl.program_id(0) == 0)
    def _():
        energy_ref[...] = jnp.zeros_like(energy_ref)
        cb, sb = cb_ref[...], sb_ref[...]
        for g in range(groups):
            ca, sa = ca_ref[g : g + 1, :], sa_ref[g : g + 1, :]
            kernel_ref[32 * g : 32 * g + 16, :] = (ca * cb - sa * sb).astype(BF16)
            kernel_ref[32 * g + 16 : 32 * (g + 1), :] = (-(sa * cb + ca * sb)).astype(BF16)

    out_ref[...] = mm(kernel_ref[...], echo_ref[...], NN)
    echo = echo_ref[...].astype(F32)
    square = jnp.sum((echo * echo).reshape(-1, 8, echo.shape[1]), axis=0)
    for j in range(square.shape[1] // 128):
        energy_ref[...] += square[:, 128 * j : 128 * (j + 1)]


def full(shape):
    return pl.BlockSpec(shape, lambda *_: (0,) * len(shape))


VMEM = pl.BlockSpec(memory_space=pltpu.VMEM)
HBM = pl.BlockSpec(memory_space=pl.ANY)


def call(body, outs, *args, scratch=(), blocked=None, blocked_out=None, steps=None, in_hbm=()):
    blocked, blocked_out = blocked or {}, blocked_out or {}
    in_specs = [blocked.get(i, VMEM) for i in range(len(args))]
    out_specs = [blocked_out.get(i, HBM if i in in_hbm else VMEM) for i in range(len(outs))]
    shapes = [
        jax.ShapeDtypeStruct(*shape) if i in blocked_out else (pltpu.HBM if i in in_hbm else pltpu.VMEM)(*shape)
        for i, shape in enumerate(outs)
    ]
    args = [
        pltpu.with_memory_space_constraint(arg, pltpu.HBM if i in blocked else pltpu.VMEM)
        for i, arg in enumerate(args)
    ]
    return pl.pallas_call(
        body, in_specs=in_specs, out_specs=out_specs, out_shape=shapes, scratch_shapes=list(scratch),
        compiler_params=pltpu.CompilerParams(vmem_limit_bytes=28 * 2**20), **({"grid": (steps,)} if steps else {}),
    )(*args)


def on_device(echoes, chirp_phase, sample_init, threshold, ridge_scale):
    groups = lax.axis_size("pulse")
    rows, cols = echoes.shape
    half = rows // 2
    cells = rows * cols * groups * lax.axis_size("sample")
    pulse_total = rows * groups
    own_pulse = lax.axis_index("pulse")
    scalars = jnp.broadcast_to(jnp.concatenate([threshold, ridge_scale] * 4)[:, None], (8, 128))
    echo3 = echoes.reshape(2, half, cols)
    across_z = [[2 * z + c for z in range(groups // 2)] for c in range(2)]
    other_core = [(i, i ^ 1) for i in range(groups)]
    stacked = [pltpu.VMEM((128, cols), BF16)] * 2
    turned = [pltpu.VMEM((cols, 128), BF16)] * 2

    bp = half // 2
    row_blocks = pl.BlockSpec((2, bp, cols), lambda i: (0, i, 0))
    to_solve = call(
        first_products, [((16, 64, 128), F32)], echo3, sample_init.T, steps=2,
        blocked={0: row_blocks, 1: full((RANK, cols))},
        blocked_out={0: pl.BlockSpec((8, 64, 128), lambda i: (i, 0, 0))},
        scratch=turned + [pltpu.VMEM((32, 128), F32)],
    )[0]
    to_solve, chirp_phase = lax.optimization_barrier((to_solve, chirp_phase))
    got = lax.all_to_all(to_solve, "sample", 0, 0, tiled=True)

    pulses = own_pulse * rows + jnp.arange(rows, dtype=jnp.int32)
    phases = lax.dynamic_slice_in_dim(chirp_phase, own_pulse * rows, rows)
    steps = jnp.arange(16, dtype=jnp.int32)[:, None]
    turn = 2.0 * jnp.pi / pulse_total
    angle_a = jnp.mod((16 * steps - BINS // 2) * pulses[None, :], pulse_total).astype(F32) * turn + phases[None, :]
    angle_b = jnp.mod(steps * pulses[None, :], pulse_total).astype(F32) * turn
    scale = 1.0 / jnp.sqrt(F32(pulse_total))
    table = full((16, rows))
    dcols = 512
    kernel, spectrum, energy = pl.pallas_call(
        doppler_products, grid=(cols // dcols,),
        in_specs=[table] * 4 + [pl.BlockSpec((rows, dcols), lambda i: (0, i))],
        out_specs=[full((2 * BINS, rows)), pl.BlockSpec((2 * BINS, dcols), lambda i: (0, i)), full((8, 128))],
        out_shape=[jax.ShapeDtypeStruct((2 * BINS, rows), BF16), jax.ShapeDtypeStruct((2 * BINS, cols), F32), jax.ShapeDtypeStruct((8, 128), F32)],
        compiler_params=pltpu.CompilerParams(vmem_limit_bytes=56 * 2**20), name="doppler_products",
    )(jnp.cos(angle_a) * scale, jnp.sin(angle_a) * scale, jnp.cos(angle_b), jnp.sin(angle_b), echoes)

    data3 = echo3
    for turn_index in range(ITERS):
        last = turn_index == ITERS - 1
        pulse_out = [((16, 32, 128), F32 if last else BF16)]
        if turn_index == 0:
            mine = call(solve_pulses, pulse_out, scalars, got)[0]
        else:
            got = lax.all_to_all(to_solve, "sample", 0, 0, tiled=True)
            block = call(invert_gram, [((128, 128), F32)], scalars, grams)[0]
            mine = call(apply_pulses, pulse_out, got, block)[0]
        u_full = lax.all_to_all(mine, "sample", 0, 0, tiled=True).reshape(half, 128)
        u_bf = u_full.astype(BF16)
        depth = RANK + 32 + (16 if last else 8)
        extra = kernel if last else energy
        keep, send = call(
            sample_products, [((8, depth, 128), F32)] * 2, data3, u_bf, extra, steps=2,
            blocked={0: pl.BlockSpec((2, half, cols // 2), lambda i: (0, 0, i)), **({2: pl.BlockSpec((BINS, rows), lambda i: (i, 0))} if last else {})},
            blocked_out={i: pl.BlockSpec((4, depth, 128), lambda i: (i, 0, 0)) for i in range(2)},
            scratch=[pltpu.VMEM((128, half), BF16)],
        )
        keep = keep + lax.ppermute(send, "pulse", other_core)
        got = lax.all_to_all(keep, "pulse", 0, 0, tiled=True, axis_index_groups=across_z)
        width = RANK if last else RANK + 16
        outs = [((16, width, 128), BF16), ((16 if last else 40, 128), F32)]
        mine = call(solve_samples, outs, scalars, got)
        v_chunks = lax.all_to_all(mine[0], "pulse", 0, 0, tiled=True)

        def direct_squares(u_bf, v_chunks, between=lambda sums: sums):
            sums = call(residual_squares, [((16, 8, 128), F32)], echo3, u_bf, v_chunks, scratch=stacked)[0]
            sums = lax.all_to_all(sums, "sample", 0, 0, tiled=True)
            sums = between(jnp.sum(sums, axis=0, keepdims=True))
            sums = lax.all_to_all(jnp.broadcast_to(sums, (16, 8, 128)), "pulse", 0, 0, tiled=True)
            return jnp.sum(sums, axis=0)

        if last:
            def between(sums):
                nonlocal spectrum
                sums, spectrum = lax.optimization_barrier((sums, spectrum))
                return sums

            sums = direct_squares(u_bf, v_chunks, between)
        else:
            v_chunks, spectrum = lax.optimization_barrier((v_chunks, spectrum))
            spectrum = lax.psum_scatter(
                spectrum.reshape(groups, 2 * BINS // groups, cols), "pulse", scatter_dimension=0, tiled=True
            )
            grams = call(sample_gram, [((16, 48, 128), F32)], v_chunks, mine[1])[0]
            grams = lax.all_to_all(grams, "sample", 0, 0, tiled=True)
            sums, total = call(squares_from_products, [((8, 128), F32)] * 2, grams, mine[1])
            if FALLBACK:
                sums = lax.cond(
                    sums[0, 0] > 0.001 * total[0, 0],
                    lambda sums, u_bf, v_chunks: sums,
                    lambda sums, u_bf, v_chunks: direct_squares(u_bf, v_chunks),
                    sums, u_bf, v_chunks,
                )
            to_solve, data3 = call(
                lambda *refs: next_products(cells, *refs),
                [((16, 32, 128), F32), (echo3.shape, BF16)],
                scalars, echo3, u_bf, v_chunks, sums, in_hbm=(1,),
                scratch=stacked + turned + [pltpu.VMEM((2, 2, bp, cols), BF16), pltpu.SemaphoreType.DMA((2, 2))],
            )
    doppler = call(correct_doppler, [((16, 2, cols), F32)], v_chunks, spectrum, mine[1])[0]
    sums, doppler = lax.optimization_barrier((sums, doppler))
    sparse = call(
        lambda *refs: finish(cells, *refs), [(echo3.shape, BF16)],
        scalars, echo3, u_bf, v_chunks, sums, steps=2, blocked={1: row_blocks}, blocked_out={0: row_blocks},
        scratch=stacked + [pltpu.VMEM((1, 128), F32)],
    )[0]
    turned_factor = u_full.T
    pulse_factor = jnp.concatenate([turned_factor[:RANK], turned_factor[RANK:]], axis=1).T
    return (doppler, pulse_factor, sparse.reshape(rows, cols))


def solution(mesh):
    placed = (P("pulse", "sample"), P(), P("sample", None), P(), P())
    return jax.shard_map(
        on_device,
        mesh=mesh,
        in_specs=placed,
        out_specs=(P("pulse", None, "sample"), P("pulse", None), P("pulse", "sample")),
        check_vma=False,
    )
```

```python
import jax
import jax.numpy as jnp
from jax import lax
from jax.experimental import pallas as pl
from jax.experimental.pallas import tpu as pltpu
from jax.sharding import PartitionSpec as P


BINS = 256
ITERS = 2
FALLBACK = True
RANK = 64
F32 = jnp.float32
BF16 = jnp.bfloat16
HIGH = lax.Precision.HIGHEST

NN = (((1,), (0,)), ((), ()))
NT = (((1,), (1,)), ((), ()))


def mm(a, b, dims):
    return lax.dot_general(a, b, dims, preferred_element_type=F32)


def mm_exact(a, b):
    return lax.dot_general(a, b, NN, precision=HIGH, preferred_element_type=F32)


def lanes_low(shape):
    return lax.broadcasted_iota(jnp.int32, shape, 1) < RANK


def pack_square(twice):
    half = RANK // 2
    return jnp.where(lanes_low((half, 128)), twice[:half], twice[half:])


def unpack_square(packed):
    swapped = pltpu.roll(packed, RANK, 1)
    low = lanes_low(packed.shape)
    return jnp.concatenate(
        [jnp.where(low, packed, swapped), jnp.where(low, swapped, packed)], axis=0
    )


def ridge_inverse(twice, ridge_scale):
    row = lax.broadcasted_iota(jnp.int32, (RANK, 128), 0)
    lane = lax.broadcasted_iota(jnp.int32, (RANK, 128), 1)
    diag = row == lane
    trace = jnp.sum(jnp.sum(jnp.where(diag, twice, 0.0), axis=0, keepdims=True), axis=1, keepdims=True)
    shift = ridge_scale * trace / RANK
    unit = (lane == row + RANK).astype(F32)
    work = jnp.where(lane < RANK, twice + jnp.where(diag, shift, 0.0), unit)
    panel = 8
    for start in range(0, RANK, panel):
        columns = [
            jnp.broadcast_to(work[:, start + j : start + j + 1], (RANK, 128)) for j in range(panel)
        ]
        for j in range(panel):
            k = start + j
            inverse = 1.0 / columns[j][k : k + 1, :]
            scaled = work[k : k + 1, :] * inverse
            for i in range(j + 1, panel):
                entry = columns[j][start + i : start + i + 1, :] * inverse
                columns[i] = jnp.where(row == k, entry, columns[i] - columns[j] * entry)
            work = jnp.where(row == k, scaled, work - columns[j] * scaled)
    swapped = pltpu.roll(work, RANK, 1)
    return jnp.where(lane < RANK, swapped, work)


def stack_factor(v_ref, va_ref, vb_ref, ta_ref=None, tb_ref=None):
    chunks, _, width = v_ref.shape
    rank = RANK
    cols = chunks * width
    va_ref[rank:, :] = jnp.zeros((rank, cols), va_ref.dtype)
    vb_ref[:rank, :] = jnp.zeros((rank, cols), vb_ref.dtype)
    for j in range(chunks):
        part = v_ref[j, :rank]
        here = slice(j * width, (j + 1) * width)
        va_ref[:rank, here] = part
        vb_ref[rank:, here] = part
        if ta_ref is not None:
            turned = jnp.concatenate([part, part], axis=0).T
            zero = jnp.zeros_like(turned)
            low = lanes_low(turned.shape)
            ta_ref[here, :] = jnp.where(low, turned, zero)
            tb_ref[here, :] = jnp.where(low, zero, turned)


def first_products(echo_ref, v_ref, out_ref, ta, tb, gram):
    @pl.when(pl.program_id(0) == 0)
    def _():
        factor = v_ref[...]
        both = jnp.concatenate([factor, factor], axis=0)
        gram[...] = pack_square(mm(factor, both, NT))
        width = 256
        low = lanes_low((width, 128))
        zero = jnp.zeros((width, 128), BF16)
        for j in range(ta.shape[0] // width):
            here = slice(j * width, (j + 1) * width)
            turned = both[:, here].T
            ta[here, :] = jnp.where(low, turned, zero)
            tb[here, :] = jnp.where(low, zero, turned)

    part = mm(echo_ref[0], ta[...], NN) + mm(echo_ref[1], tb[...], NN)
    out_ref[:, :32, :] = part.reshape(out_ref.shape[0], 32, 128)
    out_ref[:, 32:, :] = jnp.broadcast_to(gram[...][None], (out_ref.shape[0], 32, 128))


def total_of(tile):
    return jnp.sum(jnp.sum(tile, axis=0, keepdims=True), axis=1, keepdims=True)


def level_of(sums, threshold, cells):
    return threshold * jnp.sqrt(total_of(sums) / cells + 1e-06)


def next_products(cells, scalars, echo_ref, u_ref, v_ref, sums_ref, out_ref, clean_ref, va, vb, ta, tb, buffer, sems):
    stack_factor(v_ref, va, vb, ta, tb)
    copies = []
    level = level_of(sums_ref[...], scalars[0:1, 0:1], cells)
    rows = u_ref.shape[0] // 2
    for i in range(2):
        here = slice(i * rows, (i + 1) * rows)
        part = None
        for h, stacked, turned in ((0, va, ta), (1, vb, tb)):
            echo = echo_ref[h, here].astype(F32)
            residual = echo - mm(u_ref[here], stacked[...], NN)
            sparse = residual - jnp.clip(residual, -level, level)
            cleaned = (echo - sparse).astype(BF16)
            buffer[h, i] = cleaned
            copy = pltpu.make_async_copy(buffer.at[h, i], clean_ref.at[h, pl.ds(i * rows, rows)], sems.at[h, i])
            copy.start()
            copies.append(copy)
            term = mm(cleaned, turned[...], NN)
            part = term if part is None else part + term
        out_ref[8 * i : 8 * (i + 1)] = part.reshape(8, 32, 128)
    for copy in copies:
        copy.wait()


def inverse_block(twice, ridge_scale):
    inverse = ridge_inverse(twice, ridge_scale)
    low = lanes_low((RANK, 128))
    return jnp.concatenate([jnp.where(low, inverse, 0.0), jnp.where(low, 0.0, inverse)], axis=0)


def invert_gram(scalars, got_ref, out_ref):
    total = jnp.sum(got_ref[:, 16:, :], axis=0)
    out_ref[...] = inverse_block(unpack_square(total), scalars[1:2, 0:1])


def solve_pulses(scalars, got_ref, out_ref):
    total = jnp.sum(got_ref[...], axis=0)
    block = inverse_block(unpack_square(total[32:]), scalars[1:2, 0:1])
    factor = mm_exact(total[:32], block).astype(out_ref.dtype)
    out_ref[...] = jnp.broadcast_to(factor[None], out_ref.shape)


def apply_pulses(got_ref, block_ref, out_ref):
    factor = mm_exact(jnp.sum(got_ref[...], axis=0), block_ref[...]).astype(out_ref.dtype)
    out_ref[...] = jnp.broadcast_to(factor[None], out_ref.shape)


def solve_samples(scalars, got_ref, out_ref, rest_ref):
    total = jnp.sum(got_ref[...], axis=0)
    inverse = ridge_inverse(unpack_square(total[RANK : RANK + 32]), scalars[1:2, 0:1])
    factor = mm_exact(inverse[:, :RANK], total[:RANK]).astype(out_ref.dtype)
    if out_ref.shape[1] > RANK:
        inner = total_of(total[:RANK] * factor.astype(F32))
        high = inner.astype(BF16).astype(F32)
        middle = (inner - high).astype(BF16).astype(F32)
        low = inner - high - middle
        row = lax.broadcasted_iota(jnp.int32, (16, 128), 0)
        tail = jnp.where(row == 0, high, jnp.where(row == 1, middle, jnp.where(row == 2, low, 0.0)))
        factor = jnp.concatenate([factor, tail.astype(out_ref.dtype)], axis=0)
        rest_ref[...] = total[RANK:]
    else:
        rest_ref[...] = total[RANK + 32 :]
    out_ref[...] = jnp.broadcast_to(factor[None], out_ref.shape)


def sample_gram(v_ref, rest_ref, out_ref):
    chunks = v_ref.shape[0]
    square = jnp.zeros((RANK, 128), F32)
    inner = jnp.zeros((1, 1), F32)
    for j in range(chunks):
        part = v_ref[j, :RANK]
        square = square + mm(part, jnp.concatenate([part, part], axis=0), NT)
        tail = v_ref[j, RANK:].astype(F32)
        inner = inner + (tail[0:1, 0:1] + (tail[1:2, 0:1] + tail[2:3, 0:1]))
    tile = jnp.concatenate(
        [rest_ref[32:], jnp.broadcast_to(inner, (8, 128)), pack_square(square)], axis=0
    )
    out_ref[...] = jnp.broadcast_to(tile[None], out_ref.shape)


def squares_from_products(got_ref, rest_ref, sums_ref, energy_ref):
    total = jnp.sum(got_ref[...], axis=0)
    energy = total_of(total[:8])
    value = energy - 2.0 * total[8:9, 0:1] + total_of(total[16:] * rest_ref[:32])
    row = lax.broadcasted_iota(jnp.int32, (8, 128), 0)
    lane = lax.broadcasted_iota(jnp.int32, (8, 128), 1)
    sums_ref[...] = jnp.where((row == 0) & (lane == 0), value, 0.0)
    energy_ref[...] = jnp.broadcast_to(energy, (8, 128))


def sample_products(data_ref, u_ref, *refs):
    extra_ref = refs[0]
    kernel_ref = extra_ref if extra_ref.dtype == BF16 else None
    keep_ref, send_ref, turned = refs[-3:]
    width = 128
    own = lax.axis_index("pulse") % 2 == 0

    @pl.when(pl.program_id(0) == 0)
    def _():
        turned[...] = u_ref[...].T

    square = mm(turned[...], u_ref[...], NN)
    mixed = jnp.where(lanes_low((RANK, 128)), square[:RANK], square[RANK:])
    gram = pack_square(mixed + pltpu.roll(mixed, RANK, 1))
    product = mm(turned[:RANK], data_ref[0], NN) + mm(turned[RANK:], data_ref[1], NN)
    chunks = keep_ref.shape[0]
    for z in range(chunks):
        zero = product[:, 2 * z * width : (2 * z + 1) * width]
        one = product[:, (2 * z + 1) * width : (2 * z + 2) * width]
        keep_ref[z, :RANK, :] = jnp.where(own, zero, one)
        send_ref[z, :RANK, :] = jnp.where(own, one, zero)
        keep_ref[z, RANK : RANK + 32, :] = gram
        send_ref[z, RANK : RANK + 32, :] = gram
    if kernel_ref is None:
        energy = jnp.broadcast_to(extra_ref[...][None], (chunks, 8, 128))
        keep_ref[:, RANK + 32 :, :] = energy
        send_ref[:, RANK + 32 :, :] = energy
    else:
        half = kernel_ref.shape[1] // 2
        low = lanes_low((kernel_ref.shape[0], 128))
        mixed = jnp.where(
            low, mm(kernel_ref[:, :half], u_ref[...], NN), mm(kernel_ref[:, half:], u_ref[...], NN)
        )
        twice = mixed + pltpu.roll(mixed, RANK, 1)
        low = lanes_low((16, 128))
        for z in range(chunks):
            mine = twice[64 * z : 64 * (z + 1)]
            zero = jnp.where(low, mine[:16], mine[16:32])
            one = jnp.where(low, mine[32:48], mine[48:])
            keep_ref[z, RANK + 32 :, :] = jnp.where(own, zero, one)
            send_ref[z, RANK + 32 :, :] = jnp.where(own, one, zero)


def residual_squares(echo_ref, u_ref, v_ref, out_ref, va, vb):
    stack_factor(v_ref, va, vb)
    rows = u_ref.shape[0] // 2
    total = jnp.zeros((8, va.shape[1]), F32)
    for i in range(2):
        here = slice(i * rows, (i + 1) * rows)
        for h, stacked in ((0, va), (1, vb)):
            residual = echo_ref[h, here].astype(F32) - mm(u_ref[here], stacked[...], NN)
            square = residual * residual
            total = total + jnp.sum(square.reshape(-1, 8, square.shape[1]), axis=0)
    tile = total[:, :128]
    for j in range(1, total.shape[1] // 128):
        tile = tile + total[:, 128 * j : 128 * (j + 1)]
    out_ref[...] = jnp.broadcast_to(tile[None], out_ref.shape)


def add_parts(*refs):
    count = len(refs) - 6
    a_ref, b_ref = refs[:2]
    outs, (a_buf, b_buf, in_sems, out_sems) = refs[2 : 2 + count], refs[2 + count :]
    own = lax.axis_index("pulse") // 2
    loads = []
    for k in range(count):
        chunk = (own + k) % count
        pair = (
            pltpu.make_async_copy(a_ref.at[chunk], a_buf.at[k], in_sems.at[0, k]),
            pltpu.make_async_copy(b_ref.at[chunk], b_buf.at[k], in_sems.at[1, k]),
        )
        for copy in pair:
            copy.start()
        loads.append(pair)
    stores = []
    for k in range(count):
        for copy in loads[k]:
            copy.wait()
        a_buf[k] = a_buf[k] + b_buf[k]
        copy = pltpu.make_async_copy(a_buf.at[k], outs[k], out_sems.at[k])
        copy.start()
        stores.append(copy)
    for copy in stores:
        copy.wait()


def correct_doppler(v_ref, ku_ref, *refs):
    dop_refs, dop_out = refs[:-1], refs[-1]
    ku = ku_ref[...]
    high = ku.astype(BF16)
    rest = ku - high.astype(F32)
    middle = rest.astype(BF16)
    low = (rest - middle.astype(F32)).astype(BF16)
    chunks, _, width = v_ref.shape
    zero = jnp.zeros((16, RANK), BF16)
    parts = []
    for part in (high, middle, low):
        parts += [part[:, :RANK], part[:, RANK:]]
    parts = jnp.concatenate(parts, axis=0)
    for j in range(chunks):
        here = slice(j * width, (j + 1) * width)
        fix = mm(parts, v_ref[j], NN)
        fix = fix[:32] + (fix[32:64] + fix[64:])
        value = dop_refs[0][:, here]
        for dop_ref in dop_refs[1:]:
            value = value + dop_ref[:, here]
        value = value - fix
        dop_out[:, 0, here] = value[:16]
        dop_out[:, 1, here] = value[16:]


def finish(cells, scalars, echo_ref, u_ref, v_ref, sums_ref, sparse_ref, va, vb, level_ref):
    @pl.when(pl.program_id(0) == 0)
    def _():
        stack_factor(v_ref, va, vb)
        level_ref[...] = jnp.broadcast_to(level_of(sums_ref[...], scalars[0:1, 0:1], cells), (1, 128))

    level = level_ref[0:1, 0:1]
    rows = echo_ref.shape[1]
    u = u_ref[pl.ds(pl.multiple_of(pl.program_id(0) * rows, rows), rows), :]
    for h, stacked in ((0, va), (1, vb)):
        residual = echo_ref[h].astype(F32) - mm(u, stacked[...], NN)
        sparse_ref[h] = (residual - jnp.clip(residual, -level, level)).astype(BF16)


def doppler_products(ca_ref, sa_ref, cb_ref, sb_ref, echo_ref, kernel_ref, keep_ref, send_ref, energy_ref):
    groups = ca_ref.shape[0]

    @pl.when(pl.program_id(0) == 0)
    def _():
        energy_ref[...] = jnp.zeros_like(energy_ref)
        cb, sb = cb_ref[...], sb_ref[...]
        for g in range(groups):
            ca, sa = ca_ref[g : g + 1, :], sa_ref[g : g + 1, :]
            kernel_ref[32 * g : 32 * g + 16, :] = (ca * cb - sa * sb).astype(BF16)
            kernel_ref[32 * g + 16 : 32 * (g + 1), :] = (-(sa * cb + ca * sb)).astype(BF16)

    own = lax.axis_index("pulse") % 2 == 0
    product = mm(kernel_ref[...], echo_ref[...], NN)
    for z in range(keep_ref.shape[0]):
        zero, one = product[64 * z : 64 * z + 32], product[64 * z + 32 : 64 * z + 64]
        keep_ref[z] = jnp.where(own, zero, one)
        send_ref[z] = jnp.where(own, one, zero)
    echo = echo_ref[...].astype(F32)
    square = jnp.sum((echo * echo).reshape(-1, 8, echo.shape[1]), axis=0)
    for j in range(square.shape[1] // 128):
        energy_ref[...] += square[:, 128 * j : 128 * (j + 1)]


def full(shape):
    return pl.BlockSpec(shape, lambda *_: (0,) * len(shape))


VMEM = pl.BlockSpec(memory_space=pltpu.VMEM)
HBM = pl.BlockSpec(memory_space=pl.ANY)


def call(body, outs, *args, scratch=(), blocked=None, blocked_out=None, steps=None, in_hbm=()):
    blocked, blocked_out = blocked or {}, blocked_out or {}
    in_specs = [blocked.get(i, VMEM) for i in range(len(args))]
    out_specs = [blocked_out.get(i, HBM if i in in_hbm else VMEM) for i in range(len(outs))]
    shapes = [
        jax.ShapeDtypeStruct(*shape) if i in blocked_out else (pltpu.HBM if i in in_hbm else pltpu.VMEM)(*shape)
        for i, shape in enumerate(outs)
    ]
    args = [
        pltpu.with_memory_space_constraint(arg, pltpu.HBM if i in blocked else pltpu.VMEM)
        for i, arg in enumerate(args)
    ]
    return pl.pallas_call(
        body, in_specs=in_specs, out_specs=out_specs, out_shape=shapes, scratch_shapes=list(scratch),
        compiler_params=pltpu.CompilerParams(vmem_limit_bytes=28 * 2**20), **({"grid": (steps,)} if steps else {}),
    )(*args)


def on_device(echoes, chirp_phase, sample_init, threshold, ridge_scale):
    groups = lax.axis_size("pulse")
    rows, cols = echoes.shape
    half = rows // 2
    cells = rows * cols * groups * lax.axis_size("sample")
    pulse_total = rows * groups
    own_pulse = lax.axis_index("pulse")
    scalars = jnp.broadcast_to(jnp.concatenate([threshold, ridge_scale] * 4)[:, None], (8, 128))
    echo3 = echoes.reshape(2, half, cols)
    across_z = [[2 * z + c for z in range(groups // 2)] for c in range(2)]
    other_core = [(i, i ^ 1) for i in range(groups)]
    stacked = [pltpu.VMEM((128, cols), BF16)] * 2
    turned = [pltpu.VMEM((cols, 128), BF16)] * 2

    bp = half // 2
    row_blocks = pl.BlockSpec((2, bp, cols), lambda i: (0, i, 0))
    to_solve = call(
        first_products, [((16, 64, 128), F32)], echo3, sample_init.T, steps=2,
        blocked={0: row_blocks, 1: full((RANK, cols))},
        blocked_out={0: pl.BlockSpec((8, 64, 128), lambda i: (i, 0, 0))},
        scratch=turned + [pltpu.VMEM((32, 128), F32)],
    )[0]
    to_solve, chirp_phase = lax.optimization_barrier((to_solve, chirp_phase))
    got = lax.all_to_all(to_solve, "sample", 0, 0, tiled=True)

    pulses = own_pulse * rows + jnp.arange(rows, dtype=jnp.int32)
    phases = lax.dynamic_slice_in_dim(chirp_phase, own_pulse * rows, rows)
    steps = jnp.arange(16, dtype=jnp.int32)[:, None]
    turn = 2.0 * jnp.pi / pulse_total
    angle_a = jnp.mod((16 * steps - BINS // 2) * pulses[None, :], pulse_total).astype(F32) * turn + phases[None, :]
    angle_b = jnp.mod(steps * pulses[None, :], pulse_total).astype(F32) * turn
    scale = 1.0 / jnp.sqrt(F32(pulse_total))
    table = full((16, rows))
    dcols = 512
    kernel, spectrum, spectrum_sent, energy = pl.pallas_call(
        doppler_products, grid=(cols // dcols,),
        in_specs=[table] * 4 + [pl.BlockSpec((rows, dcols), lambda i: (0, i))],
        out_specs=[full((2 * BINS, rows)), *[pl.BlockSpec((groups // 2, 32, dcols), lambda i: (0, 0, i))] * 2, full((8, 128))],
        out_shape=[jax.ShapeDtypeStruct((2 * BINS, rows), BF16), *[jax.ShapeDtypeStruct((groups // 2, 32, cols), F32)] * 2, jax.ShapeDtypeStruct((8, 128), F32)],
        compiler_params=pltpu.CompilerParams(vmem_limit_bytes=56 * 2**20), name="doppler_products",
    )(jnp.cos(angle_a) * scale, jnp.sin(angle_a) * scale, jnp.cos(angle_b), jnp.sin(angle_b), echoes)

    spectrum_got = lax.ppermute(spectrum_sent, "pulse", other_core)
    ring = groups // 2
    data3 = echo3
    for turn_index in range(ITERS):
        last = turn_index == ITERS - 1
        pulse_out = [((16, 32, 128), F32 if last else BF16)]
        if turn_index == 0:
            mine = call(solve_pulses, pulse_out, scalars, got)[0]
        else:
            got = lax.all_to_all(to_solve, "sample", 0, 0, tiled=True)
            block = call(invert_gram, [((128, 128), F32)], scalars, grams)[0]
            mine = call(apply_pulses, pulse_out, got, block)[0]
        u_full = lax.all_to_all(mine, "sample", 0, 0, tiled=True).reshape(half, 128)
        u_bf = u_full.astype(BF16)
        depth = RANK + 32 + (16 if last else 8)
        extra = kernel if last else energy
        keep, send = call(
            sample_products, [((8, depth, 128), F32)] * 2, data3, u_bf, extra, steps=2,
            blocked={0: pl.BlockSpec((2, half, cols // 2), lambda i: (0, 0, i)), **({2: pl.BlockSpec((BINS, rows), lambda i: (i, 0))} if last else {})},
            blocked_out={i: pl.BlockSpec((4, depth, 128), lambda i: (i, 0, 0)) for i in range(2)},
            scratch=[pltpu.VMEM((128, half), BF16)],
        )
        keep = keep + lax.ppermute(send, "pulse", other_core)
        got = lax.all_to_all(keep, "pulse", 0, 0, tiled=True, axis_index_groups=across_z)
        width = RANK if last else RANK + 16
        outs = [((16, width, 128), BF16), ((16 if last else 40, 128), F32)]
        mine = call(solve_samples, outs, scalars, got)
        v_chunks = lax.all_to_all(mine[0], "pulse", 0, 0, tiled=True)

        def direct_squares(u_bf, v_chunks, between=lambda sums: sums):
            sums = call(residual_squares, [((16, 8, 128), F32)], echo3, u_bf, v_chunks, scratch=stacked)[0]
            sums = lax.all_to_all(sums, "sample", 0, 0, tiled=True)
            sums = between(jnp.sum(sums, axis=0, keepdims=True))
            sums = lax.all_to_all(jnp.broadcast_to(sums, (16, 8, 128)), "pulse", 0, 0, tiled=True)
            return jnp.sum(sums, axis=0)

        if last:
            def between(sums):
                nonlocal spectrum
                sums, spectrum = lax.optimization_barrier((sums, spectrum))
                return sums

            sums = direct_squares(u_bf, v_chunks, between)
        else:
            grams = call(sample_gram, [((16, 48, 128), F32)], v_chunks, mine[1])[0]
            grams = lax.all_to_all(grams, "sample", 0, 0, tiled=True)
            pieces = pl.pallas_call(
                add_parts, in_specs=[HBM] * 2, out_specs=[HBM] * ring,
                out_shape=[pltpu.HBM(spectrum.shape[1:], F32)] * ring, name="add_parts",
                scratch_shapes=[pltpu.VMEM(spectrum.shape, F32)] * 2
                + [pltpu.SemaphoreType.DMA((2, ring)), pltpu.SemaphoreType.DMA((ring,))],
                compiler_params=pltpu.CompilerParams(vmem_limit_bytes=28 * 2**20),
            )(spectrum, spectrum_got)
            spectrum = [pieces[0]]
            for step in range(1, ring):
                spectrum.append(
                    lax.ppermute(pieces[step], "pulse", [(i, (i + 2 * step) % groups) for i in range(groups)])
                )
            sums, total = call(squares_from_products, [((8, 128), F32)] * 2, grams, mine[1])
            if FALLBACK:
                sums = lax.cond(
                    sums[0, 0] > 0.001 * total[0, 0],
                    lambda sums, u_bf, v_chunks: sums,
                    lambda sums, u_bf, v_chunks: direct_squares(u_bf, v_chunks),
                    sums, u_bf, v_chunks,
                )
            to_solve, data3 = call(
                lambda *refs: next_products(cells, *refs),
                [((16, 32, 128), F32), (echo3.shape, BF16)],
                scalars, echo3, u_bf, v_chunks, sums, in_hbm=(1,),
                scratch=stacked + turned + [pltpu.VMEM((2, 2, bp, cols), BF16), pltpu.SemaphoreType.DMA((2, 2))],
            )
    doppler = call(correct_doppler, [((16, 2, cols), F32)], v_chunks, mine[1], *spectrum)[0]
    sums, doppler = lax.optimization_barrier((sums, doppler))
    sparse = call(
        lambda *refs: finish(cells, *refs), [(echo3.shape, BF16)],
        scalars, echo3, u_bf, v_chunks, sums, steps=2, blocked={1: row_blocks}, blocked_out={0: row_blocks},
        scratch=stacked + [pltpu.VMEM((1, 128), F32)],
    )[0]
    turned_factor = u_full.T
    pulse_factor = jnp.concatenate([turned_factor[:RANK], turned_factor[RANK:]], axis=1).T
    return (doppler, pulse_factor, sparse.reshape(rows, cols))


def solution(mesh):
    placed = (P("pulse", "sample"), P(), P("sample", None), P(), P())
    return jax.shard_map(
        on_device,
        mesh=mesh,
        in_specs=placed,
        out_specs=(P("pulse", None, "sample"), P("pulse", None), P("pulse", "sample")),
        check_vma=False,
    )
```

```python
import jax
import jax.numpy as jnp
from jax import lax
from jax.experimental import pallas as pl
from jax.experimental.pallas import tpu as pltpu
from jax.sharding import PartitionSpec as P


BINS = 256
ITERS = 2
FALLBACK = True
RANK = 64
F32 = jnp.float32
BF16 = jnp.bfloat16
HIGH = lax.Precision.HIGHEST

NN = (((1,), (0,)), ((), ()))
NT = (((1,), (1,)), ((), ()))


def mm(a, b, dims):
    return lax.dot_general(a, b, dims, preferred_element_type=F32)


def mm_exact(a, b):
    return lax.dot_general(a, b, NN, precision=HIGH, preferred_element_type=F32)


def lanes_low(shape):
    return lax.broadcasted_iota(jnp.int32, shape, 1) < RANK


def pack_square(twice):
    half = RANK // 2
    return jnp.where(lanes_low((half, 128)), twice[:half], twice[half:])


def unpack_square(packed):
    swapped = pltpu.roll(packed, RANK, 1)
    low = lanes_low(packed.shape)
    return jnp.concatenate(
        [jnp.where(low, packed, swapped), jnp.where(low, swapped, packed)], axis=0
    )


def ridge_inverse(twice, ridge_scale):
    row = lax.broadcasted_iota(jnp.int32, (RANK, 128), 0)
    lane = lax.broadcasted_iota(jnp.int32, (RANK, 128), 1)
    diag = row == lane
    trace = jnp.sum(jnp.sum(jnp.where(diag, twice, 0.0), axis=0, keepdims=True), axis=1, keepdims=True)
    shift = ridge_scale * trace / RANK
    unit = (lane == row + RANK).astype(F32)
    work = jnp.where(lane < RANK, twice + jnp.where(diag, shift, 0.0), unit)
    panel = 8
    for start in range(0, RANK, panel):
        columns = [
            jnp.broadcast_to(work[:, start + j : start + j + 1], (RANK, 128)) for j in range(panel)
        ]
        for j in range(panel):
            k = start + j
            inverse = 1.0 / columns[j][k : k + 1, :]
            scaled = work[k : k + 1, :] * inverse
            for i in range(j + 1, panel):
                entry = columns[j][start + i : start + i + 1, :] * inverse
                columns[i] = jnp.where(row == k, entry, columns[i] - columns[j] * entry)
            work = jnp.where(row == k, scaled, work - columns[j] * scaled)
    swapped = pltpu.roll(work, RANK, 1)
    return jnp.where(lane < RANK, swapped, work)


def stack_factor(v_ref, va_ref, vb_ref, ta_ref=None, tb_ref=None):
    chunks, _, width = v_ref.shape
    rank = RANK
    cols = chunks * width
    va_ref[rank:, :] = jnp.zeros((rank, cols), va_ref.dtype)
    vb_ref[:rank, :] = jnp.zeros((rank, cols), vb_ref.dtype)
    for j in range(chunks):
        part = v_ref[j, :rank]
        here = slice(j * width, (j + 1) * width)
        va_ref[:rank, here] = part
        vb_ref[rank:, here] = part
        if ta_ref is not None:
            turned = jnp.concatenate([part, part], axis=0).T
            zero = jnp.zeros_like(turned)
            low = lanes_low(turned.shape)
            ta_ref[here, :] = jnp.where(low, turned, zero)
            tb_ref[here, :] = jnp.where(low, zero, turned)


def first_products(echo_ref, v_ref, out_ref, ta, tb, gram):
    @pl.when(pl.program_id(0) == 0)
    def _():
        factor = v_ref[...]
        both = jnp.concatenate([factor, factor], axis=0)
        gram[...] = pack_square(mm(factor, both, NT))
        width = 256
        low = lanes_low((width, 128))
        zero = jnp.zeros((width, 128), BF16)
        for j in range(ta.shape[0] // width):
            here = slice(j * width, (j + 1) * width)
            turned = both[:, here].T
            ta[here, :] = jnp.where(low, turned, zero)
            tb[here, :] = jnp.where(low, zero, turned)

    part = mm(echo_ref[0], ta[...], NN) + mm(echo_ref[1], tb[...], NN)
    out_ref[:, :32, :] = part.reshape(out_ref.shape[0], 32, 128)
    out_ref[:, 32:, :] = jnp.broadcast_to(gram[...][None], (out_ref.shape[0], 32, 128))


def total_of(tile):
    return jnp.sum(jnp.sum(tile, axis=0, keepdims=True), axis=1, keepdims=True)


def level_of(sums, threshold, cells):
    return threshold * jnp.sqrt(total_of(sums) / cells + 1e-06)


def start_loads(echo_ref, buffer, sems):
    loads = {}
    rows = buffer.shape[2]
    for i in range(buffer.shape[1]):
        for h in range(2):
            copy = pltpu.make_async_copy(echo_ref.at[h, pl.ds(i * rows, rows)], buffer.at[h, i], sems.at[0, h, i])
            copy.start()
            loads[h, i] = copy
    return loads


def next_products(cells, scalars, echo_ref, u_ref, v_ref, sums_ref, out_ref, clean_ref, va, vb, ta, tb, buffer, sems):
    loads = start_loads(echo_ref, buffer, sems)
    stack_factor(v_ref, va, vb, ta, tb)
    level = level_of(sums_ref[...], scalars[0:1, 0:1], cells)
    rows = buffer.shape[2]
    copies = []
    for i in range(buffer.shape[1]):
        here = slice(i * rows, (i + 1) * rows)
        part = None
        for h, stacked, turned in ((0, va, ta), (1, vb, tb)):
            loads[h, i].wait()
            echo = buffer[h, i].astype(F32)
            residual = echo - mm(u_ref[here], stacked[...], NN)
            sparse = residual - jnp.clip(residual, -level, level)
            cleaned = (echo - sparse).astype(BF16)
            buffer[h, i] = cleaned
            copy = pltpu.make_async_copy(buffer.at[h, i], clean_ref.at[h, pl.ds(i * rows, rows)], sems.at[1, h, i])
            copy.start()
            copies.append(copy)
            term = mm(cleaned, turned[...], NN)
            part = term if part is None else part + term
        out_ref[(rows // 32) * i : (rows // 32) * (i + 1)] = part.reshape(rows // 32, 32, 128)
    for copy in copies:
        copy.wait()


def inverse_block(twice, ridge_scale):
    inverse = ridge_inverse(twice, ridge_scale)
    low = lanes_low((RANK, 128))
    return jnp.concatenate([jnp.where(low, inverse, 0.0), jnp.where(low, 0.0, inverse)], axis=0)


def invert_gram(scalars, got_ref, out_ref):
    total = jnp.sum(got_ref[:, 16:, :], axis=0)
    out_ref[...] = inverse_block(unpack_square(total), scalars[1:2, 0:1])


def solve_pulses(scalars, got_ref, out_ref):
    total = jnp.sum(got_ref[...], axis=0)
    block = inverse_block(unpack_square(total[32:]), scalars[1:2, 0:1])
    factor = mm_exact(total[:32], block).astype(out_ref.dtype)
    out_ref[...] = jnp.broadcast_to(factor[None], out_ref.shape)


def apply_pulses(got_ref, block_ref, out_ref):
    factor = mm_exact(jnp.sum(got_ref[...], axis=0), block_ref[...]).astype(out_ref.dtype)
    out_ref[...] = jnp.broadcast_to(factor[None], out_ref.shape)


def solve_samples(scalars, got_ref, out_ref, rest_ref):
    total = jnp.sum(got_ref[...], axis=0)
    inverse = ridge_inverse(unpack_square(total[RANK : RANK + 32]), scalars[1:2, 0:1])
    factor = mm_exact(inverse[:, :RANK], total[:RANK]).astype(out_ref.dtype)
    if out_ref.shape[1] > RANK:
        inner = total_of(total[:RANK] * factor.astype(F32))
        high = inner.astype(BF16).astype(F32)
        middle = (inner - high).astype(BF16).astype(F32)
        low = inner - high - middle
        row = lax.broadcasted_iota(jnp.int32, (16, 128), 0)
        tail = jnp.where(row == 0, high, jnp.where(row == 1, middle, jnp.where(row == 2, low, 0.0)))
        factor = jnp.concatenate([factor, tail.astype(out_ref.dtype)], axis=0)
        rest_ref[...] = total[RANK:]
    else:
        rest_ref[...] = total[RANK + 32 :]
    out_ref[...] = jnp.broadcast_to(factor[None], out_ref.shape)


def sample_gram(v_ref, rest_ref, out_ref):
    chunks = v_ref.shape[0]
    square = jnp.zeros((RANK, 128), F32)
    inner = jnp.zeros((1, 1), F32)
    for j in range(chunks):
        part = v_ref[j, :RANK]
        square = square + mm(part, jnp.concatenate([part, part], axis=0), NT)
        tail = v_ref[j, RANK:].astype(F32)
        inner = inner + (tail[0:1, 0:1] + (tail[1:2, 0:1] + tail[2:3, 0:1]))
    tile = jnp.concatenate(
        [rest_ref[32:], jnp.broadcast_to(inner, (8, 128)), pack_square(square)], axis=0
    )
    out_ref[...] = jnp.broadcast_to(tile[None], out_ref.shape)


def squares_from_products(got_ref, rest_ref, sums_ref, safe_ref):
    total = jnp.sum(got_ref[...], axis=0)
    energy = total_of(total[:8])
    value = energy - 2.0 * total[8:9, 0:1] + total_of(total[16:] * rest_ref[:32])
    row = lax.broadcasted_iota(jnp.int32, (8, 128), 0)
    lane = lax.broadcasted_iota(jnp.int32, (8, 128), 1)
    sums_ref[...] = jnp.where((row == 0) & (lane == 0), value, 0.0)
    safe_ref[...] = jnp.broadcast_to(jnp.where(value > 0.001 * energy, 1.0, 0.0), (8, 128))


def sample_products(data_ref, u_ref, *refs):
    extra_ref = refs[0]
    kernel_ref = extra_ref if extra_ref.dtype == BF16 else None
    keep_ref, send_ref, turned = refs[-3:]
    width = 128
    own = lax.axis_index("pulse") % 2 == 0

    @pl.when(pl.program_id(0) == 0)
    def _():
        turned[...] = u_ref[...].T

    square = mm(turned[...], u_ref[...], NN)
    mixed = jnp.where(lanes_low((RANK, 128)), square[:RANK], square[RANK:])
    gram = pack_square(mixed + pltpu.roll(mixed, RANK, 1))
    product = mm(turned[:RANK], data_ref[0], NN) + mm(turned[RANK:], data_ref[1], NN)
    chunks = keep_ref.shape[0]
    for z in range(chunks):
        zero = product[:, 2 * z * width : (2 * z + 1) * width]
        one = product[:, (2 * z + 1) * width : (2 * z + 2) * width]
        keep_ref[z, :RANK, :] = jnp.where(own, zero, one)
        send_ref[z, :RANK, :] = jnp.where(own, one, zero)
        keep_ref[z, RANK : RANK + 32, :] = gram
        send_ref[z, RANK : RANK + 32, :] = gram
    if kernel_ref is None:
        energy = jnp.broadcast_to(extra_ref[...][None], (chunks, 8, 128))
        keep_ref[:, RANK + 32 :, :] = energy
        send_ref[:, RANK + 32 :, :] = energy
    else:
        half = kernel_ref.shape[1] // 2
        low = lanes_low((kernel_ref.shape[0], 128))
        mixed = jnp.where(
            low, mm(kernel_ref[:, :half], u_ref[...], NN), mm(kernel_ref[:, half:], u_ref[...], NN)
        )
        twice = mixed + pltpu.roll(mixed, RANK, 1)
        low = lanes_low((16, 128))
        for z in range(chunks):
            mine = twice[64 * z : 64 * (z + 1)]
            zero = jnp.where(low, mine[:16], mine[16:32])
            one = jnp.where(low, mine[32:48], mine[48:])
            keep_ref[z, RANK + 32 :, :] = jnp.where(own, zero, one)
            send_ref[z, RANK + 32 :, :] = jnp.where(own, one, zero)


def residual_squares(echo_ref, u_ref, v_ref, out_ref, va, vb):
    stack_factor(v_ref, va, vb)
    rows = u_ref.shape[0] // 2
    total = jnp.zeros((8, va.shape[1]), F32)
    for i in range(2):
        here = slice(i * rows, (i + 1) * rows)
        for h, stacked in ((0, va), (1, vb)):
            residual = echo_ref[h, here].astype(F32) - mm(u_ref[here], stacked[...], NN)
            square = residual * residual
            total = total + jnp.sum(square.reshape(-1, 8, square.shape[1]), axis=0)
    tile = total[:, :128]
    for j in range(1, total.shape[1] // 128):
        tile = tile + total[:, 128 * j : 128 * (j + 1)]
    out_ref[...] = jnp.broadcast_to(tile[None], out_ref.shape)


def add_parts(*refs):
    count = len(refs) - 6
    a_ref, b_ref = refs[:2]
    outs, (a_buf, b_buf, in_sems, out_sems) = refs[2 : 2 + count], refs[2 + count :]
    own = lax.axis_index("pulse") // 2
    loads = []
    for k in range(count):
        chunk = (own + k) % count
        pair = (
            pltpu.make_async_copy(a_ref.at[chunk], a_buf.at[k], in_sems.at[0, k]),
            pltpu.make_async_copy(b_ref.at[chunk], b_buf.at[k], in_sems.at[1, k]),
        )
        for copy in pair:
            copy.start()
        loads.append(pair)
    stores = []
    for k in range(count):
        for copy in loads[k]:
            copy.wait()
        a_buf[k] = a_buf[k] + b_buf[k]
        copy = pltpu.make_async_copy(a_buf.at[k], outs[k], out_sems.at[k])
        copy.start()
        stores.append(copy)
    for copy in stores:
        copy.wait()


def correct_doppler(v_ref, ku_ref, *refs):
    dop_refs, (out_ref, dop_out, sems) = refs[:-3], refs[-3:]
    ku = ku_ref[...]
    high = ku.astype(BF16)
    rest = ku - high.astype(F32)
    middle = rest.astype(BF16)
    low = (rest - middle.astype(F32)).astype(BF16)
    chunks, _, width = v_ref.shape
    zero = jnp.zeros((16, RANK), BF16)
    parts = []
    for part in (high, middle, low):
        parts += [part[:, :RANK], part[:, RANK:]]
    parts = jnp.concatenate(parts, axis=0)
    for j in range(chunks):
        here = slice(j * width, (j + 1) * width)
        fix = mm(parts, v_ref[j], NN)
        fix = fix[:32] + (fix[32:64] + fix[64:])
        value = dop_refs[0][:, here]
        for dop_ref in dop_refs[1:]:
            value = value + dop_ref[:, here]
        value = value - fix
        dop_out[:, 0, here] = value[:16]
        dop_out[:, 1, here] = value[16:]
    copy = pltpu.make_async_copy(dop_out, out_ref, sems.at[0])
    copy.start()
    copy.wait()


def finish(cells, scalars, echo_ref, u_ref, v_ref, sums_ref, sparse_ref, va, vb, buffer, sems):
    loads = start_loads(echo_ref, buffer, sems)
    stack_factor(v_ref, va, vb)
    level = level_of(sums_ref[...], scalars[0:1, 0:1], cells)
    rows = buffer.shape[2]
    copies = []
    for i in range(buffer.shape[1]):
        here = slice(i * rows, (i + 1) * rows)
        for h, stacked in ((0, va), (1, vb)):
            loads[h, i].wait()
            residual = buffer[h, i].astype(F32) - mm(u_ref[here], stacked[...], NN)
            buffer[h, i] = (residual - jnp.clip(residual, -level, level)).astype(BF16)
            copy = pltpu.make_async_copy(buffer.at[h, i], sparse_ref.at[h, pl.ds(i * rows, rows)], sems.at[1, h, i])
            copy.start()
            copies.append(copy)
    for copy in copies:
        copy.wait()


def doppler_products(ca_ref, sa_ref, cb_ref, sb_ref, echo_ref, kernel_ref, keep_ref, send_ref, energy_ref):
    groups = ca_ref.shape[0]

    @pl.when(pl.program_id(0) == 0)
    def _():
        energy_ref[...] = jnp.zeros_like(energy_ref)
        cb, sb = cb_ref[...], sb_ref[...]
        for g in range(groups):
            ca, sa = ca_ref[g : g + 1, :], sa_ref[g : g + 1, :]
            kernel_ref[32 * g : 32 * g + 16, :] = (ca * cb - sa * sb).astype(BF16)
            kernel_ref[32 * g + 16 : 32 * (g + 1), :] = (-(sa * cb + ca * sb)).astype(BF16)

    own = lax.axis_index("pulse") % 2 == 0
    product = mm(kernel_ref[...], echo_ref[...], NN)
    for z in range(keep_ref.shape[0]):
        zero, one = product[64 * z : 64 * z + 32], product[64 * z + 32 : 64 * z + 64]
        keep_ref[z] = jnp.where(own, zero, one)
        send_ref[z] = jnp.where(own, one, zero)
    echo = echo_ref[...].astype(F32)
    square = jnp.sum((echo * echo).reshape(-1, 8, echo.shape[1]), axis=0)
    for j in range(square.shape[1] // 128):
        energy_ref[...] += square[:, 128 * j : 128 * (j + 1)]


def full(shape):
    return pl.BlockSpec(shape, lambda *_: (0,) * len(shape))


VMEM = pl.BlockSpec(memory_space=pltpu.VMEM)
HBM = pl.BlockSpec(memory_space=pl.ANY)


def call(body, outs, *args, scratch=(), blocked=None, blocked_out=None, steps=None, in_hbm=()):
    blocked, blocked_out = blocked or {}, blocked_out or {}
    in_specs = [blocked.get(i, VMEM) for i in range(len(args))]
    out_specs = [blocked_out.get(i, HBM if i in in_hbm else VMEM) for i in range(len(outs))]
    shapes = [
        jax.ShapeDtypeStruct(*shape) if i in blocked_out else (pltpu.HBM if i in in_hbm else pltpu.VMEM)(*shape)
        for i, shape in enumerate(outs)
    ]
    args = [
        pltpu.with_memory_space_constraint(arg, pltpu.HBM if i in blocked else pltpu.VMEM)
        for i, arg in enumerate(args)
    ]
    return pl.pallas_call(
        body, in_specs=in_specs, out_specs=out_specs, out_shape=shapes, scratch_shapes=list(scratch),
        compiler_params=pltpu.CompilerParams(vmem_limit_bytes=28 * 2**20), **({"grid": (steps,)} if steps else {}),
    )(*args)


def on_device(echoes, chirp_phase, sample_init, threshold, ridge_scale):
    groups = lax.axis_size("pulse")
    rows, cols = echoes.shape
    half = rows // 2
    cells = rows * cols * groups * lax.axis_size("sample")
    pulse_total = rows * groups
    own_pulse = lax.axis_index("pulse")
    scalars = jnp.broadcast_to(jnp.concatenate([threshold, ridge_scale] * 4)[:, None], (8, 128))
    echo3 = echoes.reshape(2, half, cols)
    across_z = [[2 * z + c for z in range(groups // 2)] for c in range(2)]
    other_core = [(i, i ^ 1) for i in range(groups)]
    stacked = [pltpu.VMEM((128, cols), BF16)] * 2
    turned = [pltpu.VMEM((cols, 128), BF16)] * 2

    bp = half // 2
    block_buffer = [pltpu.VMEM((2, 2, bp, cols), BF16), pltpu.SemaphoreType.DMA((2, 2, 2))]
    row_blocks = pl.BlockSpec((2, bp, cols), lambda i: (0, i, 0))
    to_solve = call(
        first_products, [((16, 64, 128), F32)], echo3, sample_init.T, steps=2,
        blocked={0: row_blocks, 1: full((RANK, cols))},
        blocked_out={0: pl.BlockSpec((8, 64, 128), lambda i: (i, 0, 0))},
        scratch=turned + [pltpu.VMEM((32, 128), F32)],
    )[0]
    to_solve, chirp_phase = lax.optimization_barrier((to_solve, chirp_phase))
    got = lax.all_to_all(to_solve, "sample", 0, 0, tiled=True)

    pulses = own_pulse * rows + jnp.arange(rows, dtype=jnp.int32)
    phases = lax.dynamic_slice_in_dim(chirp_phase, own_pulse * rows, rows)
    steps = jnp.arange(16, dtype=jnp.int32)[:, None]
    turn = 2.0 * jnp.pi / pulse_total
    angle_a = jnp.mod((16 * steps - BINS // 2) * pulses[None, :], pulse_total).astype(F32) * turn + phases[None, :]
    angle_b = jnp.mod(steps * pulses[None, :], pulse_total).astype(F32) * turn
    scale = 1.0 / jnp.sqrt(F32(pulse_total))
    table = full((16, rows))
    dcols = 512
    kernel, spectrum, spectrum_sent, energy = pl.pallas_call(
        doppler_products, grid=(cols // dcols,),
        in_specs=[table] * 4 + [pl.BlockSpec((rows, dcols), lambda i: (0, i))],
        out_specs=[full((2 * BINS, rows)), *[pl.BlockSpec((groups // 2, 32, dcols), lambda i: (0, 0, i))] * 2, full((8, 128))],
        out_shape=[jax.ShapeDtypeStruct((2 * BINS, rows), BF16), *[jax.ShapeDtypeStruct((groups // 2, 32, cols), F32)] * 2, jax.ShapeDtypeStruct((8, 128), F32)],
        compiler_params=pltpu.CompilerParams(vmem_limit_bytes=56 * 2**20), name="doppler_products",
    )(jnp.cos(angle_a) * scale, jnp.sin(angle_a) * scale, jnp.cos(angle_b), jnp.sin(angle_b), echoes)

    spectrum_got = lax.ppermute(spectrum_sent, "pulse", other_core)
    ring = groups // 2
    data3 = echo3
    for turn_index in range(ITERS):
        last = turn_index == ITERS - 1
        pulse_out = [((16, 32, 128), F32 if last else BF16)]
        if turn_index == 0:
            mine = call(solve_pulses, pulse_out, scalars, got)[0]
        else:
            got = lax.all_to_all(to_solve, "sample", 0, 0, tiled=True)
            block = call(invert_gram, [((128, 128), F32)], scalars, grams)[0]
            mine = call(apply_pulses, pulse_out, got, block)[0]
        u_full = lax.all_to_all(mine, "sample", 0, 0, tiled=True).reshape(half, 128)
        u_bf = u_full.astype(BF16)
        depth = RANK + 32 + (16 if last else 8)
        extra = kernel if last else energy
        keep, send = call(
            sample_products, [((8, depth, 128), F32)] * 2, data3, u_bf, extra, steps=2,
            blocked={0: pl.BlockSpec((2, half, cols // 2), lambda i: (0, 0, i)), **({2: pl.BlockSpec((BINS, rows), lambda i: (i, 0))} if last else {})},
            blocked_out={i: pl.BlockSpec((4, depth, 128), lambda i: (i, 0, 0)) for i in range(2)},
            scratch=[pltpu.VMEM((128, half), BF16)],
        )
        keep = keep + lax.ppermute(send, "pulse", other_core)
        got = lax.all_to_all(keep, "pulse", 0, 0, tiled=True, axis_index_groups=across_z)
        width = RANK if last else RANK + 16
        outs = [((16, width, 128), BF16), ((16 if last else 40, 128), F32)]
        mine = call(solve_samples, outs, scalars, got)
        v_chunks = lax.all_to_all(mine[0], "pulse", 0, 0, tiled=True)

        def direct_squares(u_bf, v_chunks, between=lambda sums: sums):
            sums = call(residual_squares, [((16, 8, 128), F32)], echo3, u_bf, v_chunks, scratch=stacked)[0]
            sums = lax.all_to_all(sums, "sample", 0, 0, tiled=True)
            sums = between(jnp.sum(sums, axis=0, keepdims=True))
            sums = lax.all_to_all(jnp.broadcast_to(sums, (16, 8, 128)), "pulse", 0, 0, tiled=True)
            return jnp.sum(sums, axis=0)

        if last:
            def between(sums):
                nonlocal spectrum
                sums, spectrum = lax.optimization_barrier((sums, spectrum))
                return sums

            sums = direct_squares(u_bf, v_chunks, between)
        else:
            grams = call(sample_gram, [((16, 48, 128), F32)], v_chunks, mine[1])[0]
            grams = lax.all_to_all(grams, "sample", 0, 0, tiled=True)
            pieces = pl.pallas_call(
                add_parts, in_specs=[HBM] * 2, out_specs=[HBM] * ring,
                out_shape=[pltpu.HBM(spectrum.shape[1:], F32)] * ring, name="add_parts",
                scratch_shapes=[pltpu.VMEM(spectrum.shape, F32)] * 2
                + [pltpu.SemaphoreType.DMA((2, ring)), pltpu.SemaphoreType.DMA((ring,))],
                compiler_params=pltpu.CompilerParams(vmem_limit_bytes=28 * 2**20),
            )(spectrum, spectrum_got)
            spectrum = [pieces[0]]
            for step in range(1, ring):
                spectrum.append(
                    lax.ppermute(pieces[step], "pulse", [(i, (i + 2 * step) % groups) for i in range(groups)])
                )
            sums, safe = call(squares_from_products, [((8, 128), F32)] * 2, grams, mine[1])
            if FALLBACK:
                sums = lax.cond(
                    safe[0, 0] > 0.5,
                    lambda sums, u_bf, v_chunks: sums,
                    lambda sums, u_bf, v_chunks: direct_squares(u_bf, v_chunks),
                    sums, u_bf, v_chunks,
                )
            to_solve, data3 = call(
                lambda *refs: next_products(cells, *refs),
                [((16, 32, 128), F32), (echo3.shape, BF16)],
                scalars, echo3, u_bf, v_chunks, sums, blocked={1: HBM}, in_hbm=(1,),
                scratch=stacked + turned + block_buffer,
            )
    doppler = call(
        correct_doppler, [((16, 2, cols), F32)], v_chunks, mine[1], *spectrum, in_hbm=(0,),
        scratch=[pltpu.VMEM((16, 2, cols), F32), pltpu.SemaphoreType.DMA((1,))],
    )[0]
    sums, doppler = lax.optimization_barrier((sums, doppler))
    sparse = call(
        lambda *refs: finish(cells, *refs), [(echo3.shape, BF16)],
        scalars, echo3, u_bf, v_chunks, sums, blocked={1: HBM}, in_hbm=(0,), scratch=stacked + block_buffer,
    )[0]
    turned_factor = u_full.T
    pulse_factor = jnp.concatenate([turned_factor[:RANK], turned_factor[RANK:]], axis=1).T
    return (doppler, pulse_factor, sparse.reshape(rows, cols))


def solution(mesh):
    placed = (P("pulse", "sample"), P(), P("sample", None), P(), P())
    return jax.shard_map(
        on_device,
        mesh=mesh,
        in_specs=placed,
        out_specs=(P("pulse", None, "sample"), P("pulse", None), P("pulse", "sample")),
        check_vma=False,
    )
```
